512 devices in a mesh: patch: 64 (over z, x, core), lev: 8 (over y).
Axes of the slice: x: 4, y: 8, z: 8, core: 2. Of those that a mesh axis runs over, the one named last changes fastest.
Arguments:
- fields: bfloat16 [8, 128, 131072], P(None, 'lev', 'patch'), may hold values from -6 to 6
- interp: bfloat16 [512, 128, 256], P('patch'), may hold values from -0.375 to 0.375
- conv_weight: bfloat16 [512, 8, 128, 128], P('patch'), may hold values from -0.1875 to 0.1875
- vert_weight: float32 [128, 5], replicated, may hold values from 0.1 to 0.5
- send_tiles: int32 [64, 4, 2], P('patch'), may hold values from 0 to 8, as said below
- tile_pattern: int32 [512, 8], P('patch'), may hold values from 0 to 15, as said below
Outputs:
- localized: float32 [8, 128, 131072], P(None, 'lev', 'patch')
The draws below stay inside these ranges and needn't reach their ends.
Inputs may be any that keep to these rules, and one draw needn't show every extreme that they name: `send_tiles`: in every draw some link carries 2 tiles; every link carries at least one tile; the tiles of one link are distinct. `tile_pattern`: each row names distinct entries, each an own tile or a filled received slot.
All inputs are finite; a program needn't handle non-finite values.
Results may differ from the reference program's by a relative error of at most 0.0048.
Values may be sent and summed in bfloat16 or wider, within the bound.
No kernel may reach another device: no remote copies, remote signals or barrier semaphores. Data moves between devices by JAX's collectives and lax.ppermute only.
A program may use at most 64 MiB of HBM per device.

```python
import math
import jax
import jax.numpy as jnp
from jax import lax

MEMBERS = 8
TILES_DEV = 8
TILE = 128
FINE_TILE = 256
K = 8
REACH = 2
MOST = 2
VHALF = 2
LEVELS = 128
BLOCKS = 512
COLUMNS = 131072
N_PATCH = 64


def link_table():
    return jnp.array([position - REACH if position < REACH else position - REACH + 1 for position in range(2 * REACH)], jnp.int32)


def link_counts(key):
    base = jax.random.fold_in(key, 11)
    counts = jax.random.randint(jax.random.fold_in(base, 1), (N_PATCH * 2 * REACH,), 1, MOST + 1)
    picked = jax.random.randint(jax.random.fold_in(base, 2), (), 0, N_PATCH * 2 * REACH)
    counts = jnp.where(jnp.arange(N_PATCH * 2 * REACH) == picked, MOST, counts)
    return counts.reshape(N_PATCH, 2 * REACH).astype(jnp.int32)


def draw_send_tiles(key, part):
    counts = link_counts(key)
    keys = jax.random.split(jax.random.fold_in(key, 12), N_PATCH * 2 * REACH)
    chosen = jax.vmap(lambda single: jax.random.permutation(single, TILES_DEV))(keys)[:, :MOST]
    chosen = chosen.reshape(N_PATCH, 2 * REACH, MOST)
    slot_ids = jnp.arange(MOST)[None, None, :]
    return jnp.where(slot_ids < counts[:, :, None], chosen, TILES_DEV).astype(jnp.int32)


def draw_tile_pattern(key, part):
    counts = link_counts(key)
    links = link_table()
    source = (jnp.arange(N_PATCH)[:, None] - links[None, :]) % N_PATCH
    arrived = counts[source, jnp.arange(2 * REACH)[None, :]]
    filled = jnp.arange(MOST)[None, None, :] < arrived[:, :, None]
    valid = jnp.concatenate([jnp.ones((N_PATCH, TILES_DEV), bool), filled.reshape(N_PATCH, 2 * REACH * MOST)], axis=1)
    width = TILES_DEV + 2 * REACH * MOST
    scores = jax.random.randint(jax.random.fold_in(key, 13), (N_PATCH, TILES_DEV, width), 0, 1 << 20) * width + jnp.arange(width)[None, None, :]
    scores = jnp.where(valid[:, None, :], scores, scores + (1 << 20) * width)
    order = jnp.argsort(scores, axis=-1)[..., :K]
    return order.reshape(N_PATCH * TILES_DEV, K).astype(jnp.int32)


def block_levels(stream_key, dims, shards, low, high):
    def one(dim, shards_of):
        heights = jax.random.uniform(jax.random.fold_in(jax.random.fold_in(stream_key, 6), dim), (shards_of,), jnp.float32, low / len(shards), high / len(shards))
        return jnp.repeat(jnp.exp(heights), dims[dim] // shards_of).reshape((-1,) + (1,) * (len(dims) - dim - 1))

    gain = one(*shards[0])
    for cut in shards[1:]:
        gain = gain * one(*cut)
    return gain


def noise(stream_key, extent, deviation, reach, cuts=(), kind=jnp.bfloat16):
    values = jax.random.normal(stream_key, extent, jnp.float32) * deviation
    if len(cuts) > 0:
        values = block_levels(stream_key, extent, cuts, -0.22, 0.18) * values
    return jnp.clip(values, min=-reach, max=reach).astype(kind)


def setup_inputs(seed: int = 0) -> dict:
    key_list = jax.random.split(jax.random.key(seed), 7)
    return {
        "fields": noise(key_list[0], (MEMBERS, LEVELS, COLUMNS), 1.0, 6.0, ((1, 8), (2, 64))),
        "interp": noise(key_list[1], (BLOCKS, TILE, FINE_TILE), FINE_TILE ** -0.5, 0.375, ((0, 64),)),
        "conv_weight": noise(key_list[2], (BLOCKS, K, TILE, TILE), (K * TILE) ** -0.5, 0.1875, ((0, 64),)),
        "vert_weight": jnp.clip(jnp.exp(jax.random.uniform(key_list[3], (LEVELS, 2 * VHALF + 1), jnp.float32, math.log(0.1), math.log(0.5))), 0.1, 0.5),
        "send_tiles": draw_send_tiles(jax.random.fold_in(key_list[6], 71), 0),
        "tile_pattern": draw_tile_pattern(jax.random.fold_in(key_list[6], 71), 0),
    }


HIGHEST = lax.Precision.HIGHEST


def link_offsets(reach_len):
    return [position - reach_len if position < reach_len else position - reach_len + 1 for position in range(2 * reach_len)]


def vertical_adjoint(values, weights, length, half_width):
    summed = jnp.zeros(values.shape[:-2] + (length, values.shape[-1]), jnp.float32)
    for offset in range(-half_width, half_width + 1):
        factor = weights[half_width + offset: half_width + offset + length, half_width - offset]
        summed = summed + factor[:, None] * values[..., half_width + offset: half_width + offset + length, :].astype(jnp.float32)
    return summed


def vertical_forward(values, weights, length, half_width):
    summed = jnp.zeros(values.shape[:-2] + (length, values.shape[-1]), jnp.float32)
    for offset in range(2 * half_width + 1):
        factor = weights[half_width: half_width + length, offset]
        summed = summed + factor[:, None] * values[..., offset: offset + length, :].astype(jnp.float32)
    return summed


def reference(fields, interp, conv_weight, vert_weight, send_tiles, tile_pattern):
    members, level_total, column_total = fields.shape
    block_total, tile_len, fine_len = interp.shape
    patch_count = N_PATCH
    tile_count = block_total // patch_count
    reach_len = send_tiles.shape[1] // 2
    slot_most = send_tiles.shape[2]
    half_width = (vert_weight.shape[1] - 1) // 2
    row_count = members * level_total
    extended_len = tile_count + 2 * reach_len * slot_most
    offsets = link_offsets(reach_len)
    flat = fields.reshape(row_count, patch_count, tile_count, fine_len)
    interp_patch = interp.reshape(patch_count, tile_count, tile_len, fine_len)
    conv_patch = conv_weight.reshape(patch_count, tile_count, -1, tile_len, tile_len)
    pattern_patch = tile_pattern.reshape(patch_count, tile_count, -1)
    positions = jnp.arange(patch_count).astype(jnp.int32)

    def restrict(position):
        block = lax.dynamic_index_in_dim(flat, position, 1, keepdims=False)
        return jnp.einsum("rtf,tcf->trc", block.astype(jnp.float32), interp_patch[position].astype(jnp.float32), precision=HIGHEST).astype(jnp.bfloat16)

    coarse = lax.map(restrict, positions)

    def adjoint_patch(position):
        products = jnp.einsum("tro,tkio->tkri", coarse[position].astype(jnp.float32), conv_patch[position].astype(jnp.float32), precision=HIGHEST)
        chosen = (pattern_patch[position][:, :, None] == jnp.arange(extended_len).astype(jnp.int32)[None, None, :]).astype(jnp.float32)
        summed = jnp.einsum("tke,tkri->eri", chosen, products, precision=HIGHEST)
        returning = summed[tile_count:].reshape(2 * reach_len, slot_most, row_count, tile_len).astype(jnp.bfloat16)
        return summed[:tile_count], returning

    own_part, returning = lax.map(adjoint_patch, positions)
    arrived_back = jnp.stack([jnp.roll(returning[:, position], -offsets[position], axis=0) for position in range(2 * reach_len)], axis=1)

    def combine(position):
        sending = (send_tiles[position][:, :, None] == jnp.arange(tile_count).astype(jnp.int32)[None, None, :]).astype(jnp.float32)
        added = jnp.einsum("ost,osri->tri", sending, arrived_back[position].astype(jnp.float32), precision=HIGHEST)
        return (own_part[position] + added).astype(jnp.bfloat16)

    adjoint = lax.map(combine, positions).reshape(patch_count, tile_count, members, level_total, tile_len)
    level_pad = ((0, 0), (0, 0), (0, 0), (half_width, half_width), (0, 0))
    weight_pad = jnp.pad(vert_weight, ((half_width, half_width), (0, 0)))
    middle = vertical_adjoint(jnp.pad(adjoint, level_pad), weight_pad, level_total, half_width).astype(jnp.bfloat16)
    smooth = vertical_forward(jnp.pad(middle, level_pad), weight_pad, level_total, half_width).astype(jnp.bfloat16)
    smooth = smooth.reshape(patch_count, tile_count, row_count, tile_len)

    def pack(position):
        sending = (send_tiles[position][:, :, None] == jnp.arange(tile_count).astype(jnp.int32)[None, None, :]).astype(jnp.float32)
        return jnp.einsum("ost,tri->osri", sending, smooth[position].astype(jnp.float32), precision=HIGHEST).astype(jnp.bfloat16)

    slots = lax.map(pack, positions)
    arrived = jnp.stack([jnp.roll(slots[:, position], offsets[position], axis=0) for position in range(2 * reach_len)], axis=1)

    def forward_patch(position):
        extended = jnp.concatenate([smooth[position], arrived[position].reshape(-1, row_count, tile_len)], axis=0)
        chosen = (pattern_patch[position][:, :, None] == jnp.arange(extended_len).astype(jnp.int32)[None, None, :]).astype(jnp.float32)
        picked = jnp.einsum("tke,eri->tkri", chosen, extended.astype(jnp.float32), precision=HIGHEST)
        mixed = jnp.einsum("tkri,tkio->tro", picked, conv_patch[position].astype(jnp.float32), precision=HIGHEST).astype(jnp.bfloat16)
        return jnp.einsum("tro,tof->rtf", mixed.astype(jnp.float32), interp_patch[position].astype(jnp.float32), precision=HIGHEST)

    result = lax.map(forward_patch, positions)
    return jnp.transpose(result, (1, 0, 2, 3)).reshape(members, level_total, column_total)
```

```python
import jax
import jax.numpy as jnp
from jax import lax
from jax.experimental import pallas as pl
from jax.experimental.pallas import tpu as pltpu
from jax.sharding import PartitionSpec as P

BF16 = jnp.bfloat16
F32 = jnp.float32
HIGHEST = lax.Precision.HIGHEST


def nn(a, b):
    return lax.dot_general(a, b, (((1,), (0,)), ((), ())), preferred_element_type=F32)


def nt(a, b):
    return lax.dot_general(a, b, (((1,), (1,)), ((), ())), preferred_element_type=F32)


def iota(shape, dim):
    return lax.broadcasted_iota(jnp.int32, shape, dim)


def split(a):
    high = a.astype(BF16)
    return high, (a - high.astype(F32)).astype(BF16)


def restrict_kernel(members, level_len, halo, fields, interp, weights, partial, halo_matrix):
    tiles, tile_len, fine = interp.shape
    rows = members * level_len
    halo_rows = members * halo
    levels, taps = weights.shape
    half = taps // 2
    start = lax.axis_index("lev") * level_len
    distance = iota((levels, levels), 1) - iota((levels, levels), 0)
    table = weights[...]
    band = jnp.zeros((levels, levels), F32)
    for j in range(taps):
        band = band + jnp.where(distance == j - half, table[:, j : j + 1], 0.0)
    both = lax.dot_general(
        band, band, (((1,), (1,)), ((), ())), precision=HIGHEST, preferred_element_type=F32
    )
    pick = (
        iota((rows, levels), 1) == start + iota((rows, levels), 0) % level_len
    ).astype(BF16)
    place = iota((2 * halo_rows, levels), 0)
    level = jnp.where(
        place < halo_rows, start - halo + place % halo, start + level_len + place % halo
    )
    pick_halo = (iota((2 * halo_rows, levels), 1) == level).astype(BF16)
    same = iota((rows, rows), 0) // level_len == iota((rows, rows), 1) // level_len
    column = iota((rows, 2 * halo_rows), 1) % halo_rows
    same_halo = iota((rows, 2 * halo_rows), 0) // level_len == column // halo
    own_parts = []
    for i, part in enumerate(split(both)):
        chosen = nn(pick, part).astype(BF16)
        own_parts.append(jnp.where(same, nt(chosen, pick), 0.0).astype(BF16))
        halo_matrix[:, i * 2 * halo_rows : (i + 1) * 2 * halo_rows] = jnp.where(
            same_halo, nt(chosen, pick_halo), 0.0
        ).astype(BF16)
    own_matrix = jnp.concatenate(own_parts, axis=1)
    for t in range(tiles):
        block = fields[:, :, t * fine : (t + 1) * fine].reshape(rows, fine)
        coarse = nt(block, interp[t]).astype(BF16)
        partial[t] = nn(own_matrix, jnp.concatenate([coarse, coarse], axis=0))


def adjoint_kernel(
    pattern, partial, halo_matrix, low, high, interp, conv, own, up, down, entries
):
    tiles, tile_len, fine = interp.shape
    count = conv.shape[1]
    entries[...] = jnp.zeros_like(entries)
    matrix = halo_matrix[...]
    for t in range(tiles):
        span = slice(t * fine, (t + 1) * fine)
        block = jnp.concatenate([low[:, span], high[:, span]], axis=0)
        edge = nt(block, interp[t]).astype(BF16)
        smooth = partial[t] + nn(matrix, jnp.concatenate([edge, edge], axis=0))
        products = nt(
            smooth.astype(BF16), conv[t].reshape(count * tile_len, tile_len)
        )
        for k in range(count):
            entry = pattern[t, k]
            entries[entry] += products[:, k * tile_len : (k + 1) * tile_len]
    own[...] = entries[:tiles]
    up[...] = entries[tiles : tiles + 4].astype(BF16)
    down[0:2] = entries[tiles + 6 : tiles + 8].astype(BF16)
    down[2:4] = entries[tiles + 4 : tiles + 6].astype(BF16)


def add_to(total, tile, piece):
    @pl.when(tile < total.shape[0])
    def _():
        total[tile] += piece.astype(F32)


def partner_kernel(send, own, up, down, from_low, from_high, total, payload):
    tiles = own.shape[0]
    core = lax.axis_index("patch") % 2
    total[...] = own[...]
    for s in range(2):
        add_to(total, send[0, 0, s], from_low[s])
        add_to(total, send[0, 3, s], from_high[s])

    @pl.when(core == 0)
    def _():
        payload[0:2] = up[2:4]
        payload[2:4] = from_high[2:4]

    @pl.when(core == 1)
    def _():
        payload[0:2] = from_low[2:4]
        payload[2:4] = down[2:4]

    for o in range(2):
        for s in range(2):
            tile = send[0, 1 + o, s]
            payload[4 + 2 * o + s] = total[jnp.minimum(tile, tiles - 1)].astype(BF16)
            payload[8, 16 * (2 * o + s) : 16 * (2 * o + s) + 16, :] = jnp.full(
                (16, payload.shape[2]), tile.astype(F32)
            ).astype(BF16)


def complete_kernel(send, partial, payload, arrived, smooth, up, down, total):
    tiles = partial.shape[0]
    total[...] = partial[...]
    for o in range(2):
        for s in range(2):
            add_to(total, send[0, 1 + o, s], arrived[2 * o + s])
    smooth[...] = total[...].astype(BF16)
    for s in range(2):
        down[s] = smooth[jnp.minimum(send[0, 0, s], tiles - 1)]
        up[s] = smooth[jnp.minimum(send[0, 3, s], tiles - 1)]
    marks = [arrived[8, 16 * i : 16 * i + 1, :].astype(F32) for i in range(4)]
    for o in range(2):
        out = (down, up)[o]
        for s in range(2):
            mine = 2 * o + s
            tile = arrived[4 + mine].astype(F32) + payload[mine].astype(F32)
            for other in range(2):
                theirs = 2 * (1 - o) + other
                tile = tile + jnp.where(
                    marks[mine] == marks[theirs], payload[theirs].astype(F32), 0.0
                )
            out[2 + s] = tile.astype(BF16)


def forward_kernel(
    pattern, smooth, up, down, from_low, from_high, interp, conv, out, entries
):
    tiles, tile_len, fine = interp.shape
    count = conv.shape[1]
    members, level_len, _ = out.shape
    core = lax.axis_index("patch") % 2
    entries[0:tiles] = smooth[...]
    entries[tiles : tiles + 2] = from_high[0:2]
    entries[tiles + 6 : tiles + 8] = from_low[0:2]

    @pl.when(core == 0)
    def _():
        entries[tiles + 2 : tiles + 4] = down[2:4]
        entries[tiles + 4 : tiles + 6] = from_low[2:4]

    @pl.when(core == 1)
    def _():
        entries[tiles + 2 : tiles + 4] = from_high[2:4]
        entries[tiles + 4 : tiles + 6] = up[2:4]

    for t in range(tiles):
        picked = jnp.concatenate([entries[pattern[t, k]] for k in range(count)], axis=1)
        mixed = nn(picked, conv[t].reshape(count * tile_len, tile_len)).astype(BF16)
        out[:, :, t * fine : (t + 1) * fine] = nn(mixed, interp[t]).reshape(
            members, level_len, fine
        )


def call(kernel, outs, ins, smem, scratch=(), flops=1 << 24):
    def spec(i):
        return pl.BlockSpec(memory_space=pltpu.SMEM if i < smem else pltpu.VMEM)

    return pl.pallas_call(
        kernel,
        out_shape=outs,
        in_specs=[spec(i) for i in range(len(ins))],
        out_specs=jax.tree.map(lambda _: pl.BlockSpec(memory_space=pltpu.VMEM), outs),
        scratch_shapes=list(scratch),
        compiler_params=pltpu.CompilerParams(vmem_limit_bytes=32 << 20),
        cost_estimate=pl.CostEstimate(flops=flops, bytes_accessed=1 << 20, transcendentals=0),
    )(*ins)


def shape(dims, dtype):
    return jax.ShapeDtypeStruct(dims, dtype)


def shards(fields, interp, conv_weight, vert_weight, send_tiles, tile_pattern):
    members, level_len, columns = fields.shape
    tiles, tile_len, fine = interp.shape
    halo = vert_weight.shape[1] - 1
    rows = members * level_len
    patches = lax.axis_size("patch")
    levs = lax.axis_size("lev")

    def shift(block, distance):
        return lax.ppermute(
            block, "patch", [(i, (i + distance) % patches) for i in range(patches)]
        )

    upward = [(i, i + 1) for i in range(levs - 1)]
    downward = [(i + 1, i) for i in range(levs - 1)]
    low = lax.ppermute(
        fields[:, level_len - halo :, :].reshape(members * halo, columns), "lev", upward
    )
    high = lax.ppermute(fields[:, :halo, :].reshape(members * halo, columns), "lev", downward)

    def restrict_body(*refs):
        restrict_kernel(members, level_len, halo, *refs)

    tile_shape = (rows, tile_len)
    partial, halo_matrix = call(
        restrict_body,
        (
            shape((tiles,) + tile_shape, F32),
            shape((rows, 4 * members * halo), BF16),
        ),
        (fields, interp, vert_weight),
        0,
    )
    four = shape((4,) + tile_shape, BF16)
    own, up, down = call(
        adjoint_kernel,
        (shape((tiles,) + tile_shape, F32), four, four),
        (tile_pattern, partial, halo_matrix, low, high, interp, conv_weight),
        1,
        [pltpu.VMEM((tiles + 8,) + tile_shape, F32)],
    )
    from_low = shift(up, 2)
    from_high = shift(down, -2)

    total, payload = call(
        partner_kernel,
        (shape((tiles,) + tile_shape, F32), shape((9,) + tile_shape, BF16)),
        (send_tiles, own, up, down, from_low, from_high),
        1,
    )
    arrived = lax.ppermute(payload, "patch", [(i, i ^ 1) for i in range(patches)])
    smooth, up, down = call(
        complete_kernel,
        (shape((tiles,) + tile_shape, BF16), four, four),
        (send_tiles, total, payload, arrived),
        1,
        [pltpu.VMEM((tiles,) + tile_shape, F32)],
    )
    from_low = shift(up, 2)
    from_high = shift(down, -2)
    return call(
        forward_kernel,
        shape(fields.shape, F32),
        (tile_pattern, smooth, up, down, from_low, from_high, interp, conv_weight),
        1,
        [pltpu.VMEM((tiles + 8,) + tile_shape, BF16)],
    )


def solution(mesh):
    in_specs = (
        P(None, "lev", "patch"),
        P("patch", None, None),
        P("patch", None, None, None),
        P(),
        P("patch", None, None),
        P("patch", None),
    )
    out_specs = P(None, "lev", "patch")
    return jax.shard_map(shards, mesh=mesh, in_specs=in_specs, out_specs=out_specs, check_vma=False)
```

```python
import functools

import jax
import jax.numpy as jnp
from jax import lax
from jax.experimental import pallas as pl
from jax.experimental.pallas import tpu as pltpu
from jax.sharding import PartitionSpec as P

BF16 = jnp.bfloat16
F32 = jnp.float32
HIGHEST = lax.Precision.HIGHEST


def nn(a, b):
    return lax.dot_general(a, b, (((1,), (0,)), ((), ())), preferred_element_type=F32)


def nt(a, b):
    return lax.dot_general(a, b, (((1,), (1,)), ((), ())), preferred_element_type=F32)


def iota(shape, dim):
    return lax.broadcasted_iota(jnp.int32, shape, dim)


def split(a):
    high = a.astype(BF16)
    return high, (a - high.astype(F32)).astype(BF16)


def restrict_kernel(halo, fields, interp, coarse, top, bottom, blocks, bases, sems):
    tiles, tile_len, fine = bases.shape
    members, level_len, _ = blocks.shape[1:]
    rows = members * level_len
    halo_rows = members * halo
    copies = []
    for t in range(tiles):
        pair = (
            pltpu.make_async_copy(
                fields.at[:, :, pl.ds(t * fine, fine)], blocks.at[t], sems.at[0, t]
            ),
            pltpu.make_async_copy(interp.at[t], bases.at[t], sems.at[1, t]),
        )
        for copy in pair:
            copy.start()
        copies.append(pair)
    place = iota((2 * halo_rows, rows), 0)
    level = jnp.where(place < halo_rows, place % halo, level_len - halo + place % halo)
    source = (place % halo_rows) // halo * level_len + level
    pick = (iota((2 * halo_rows, rows), 1) == source).astype(BF16)
    for t in range(tiles):
        for copy in copies[t]:
            copy.wait()
        value = nt(blocks[t].reshape(rows, fine), bases[t]).astype(BF16)
        coarse[t] = value
        edge = nn(pick, value).astype(BF16)
        bottom[t] = edge[:halo_rows]
        top[t] = edge[halo_rows:]


def vertical_kernel(
    level_len, halo, coarse, weights, pattern, conv, partial, halo_matrix, pattern_copy,
    conv_copy, sem
):
    fetch = pltpu.make_async_copy(conv, conv_copy, sem)
    fetch.start()
    tiles, rows, tile_len = coarse.shape
    halo_rows = rows // level_len * halo
    levels, taps = weights.shape
    half = taps // 2
    pattern_copy[...] = pattern[...]
    start = lax.axis_index("lev") * level_len
    distance = iota((levels, levels), 1) - iota((levels, levels), 0)
    table = weights[...]
    band = jnp.zeros((levels, levels), F32)
    for j in range(taps):
        band = band + jnp.where(distance == j - half, table[:, j : j + 1], 0.0)
    both = lax.dot_general(
        band, band, (((1,), (1,)), ((), ())), precision=HIGHEST, preferred_element_type=F32
    )
    pick = (
        iota((rows, levels), 1) == start + iota((rows, levels), 0) % level_len
    ).astype(BF16)
    place = iota((2 * halo_rows, levels), 0)
    level = jnp.where(
        place < halo_rows, start - halo + place % halo, start + level_len + place % halo
    )
    pick_halo = (iota((2 * halo_rows, levels), 1) == level).astype(BF16)
    same = iota((rows, rows), 0) // level_len == iota((rows, rows), 1) // level_len
    column = iota((rows, 2 * halo_rows), 1) % halo_rows
    same_halo = iota((rows, 2 * halo_rows), 0) // level_len == column // halo
    own_parts = []
    for i, part in enumerate(split(both)):
        chosen = nn(pick, part).astype(BF16)
        own_parts.append(jnp.where(same, nt(chosen, pick), 0.0).astype(BF16))
        halo_matrix[:, i * 2 * halo_rows : (i + 1) * 2 * halo_rows] = jnp.where(
            same_halo, nt(chosen, pick_halo), 0.0
        ).astype(BF16)
    own_matrix = jnp.concatenate(own_parts, axis=1)
    for t in range(tiles):
        value = coarse[t]
        partial[t] = nn(own_matrix, jnp.concatenate([value, value], axis=0))
    fetch.wait()


def by_chip(body, first, second):
    odd = lax.axis_index("patch") // 2 % 2

    @pl.when(odd == 0)
    def _():
        body(second, first)

    @pl.when(odd == 1)
    def _():
        body(first, second)


def adjoint_kernel(pattern, partial, halo_matrix, low, high, conv, own, second, first, entries):
    tiles, rows, tile_len = partial.shape
    count = conv.shape[1]
    entries[...] = jnp.zeros_like(entries)
    matrix = halo_matrix[...]
    for t in range(tiles):
        edge = jnp.concatenate([low[t], high[t]], axis=0)
        smooth = partial[t] + nn(matrix, jnp.concatenate([edge, edge], axis=0))
        products = nt(
            smooth.astype(BF16), conv[t].reshape(count * tile_len, tile_len)
        )
        for k in range(count):
            entry = pattern[t, k]
            entries[entry] += products[:, k * tile_len : (k + 1) * tile_len]
    own[...] = entries[:tiles]

    def sides(down, up):
        up[...] = entries[tiles : tiles + 4].astype(BF16)
        down[0:2] = entries[tiles + 6 : tiles + 8].astype(BF16)
        down[2:4] = entries[tiles + 4 : tiles + 6].astype(BF16)

    by_chip(sides, first, second)


def add_to(total, tile, piece):
    @pl.when(tile < total.shape[0])
    def _():
        total[tile] += piece.astype(F32)


def partner_kernel(send, own, first, second, from_first, from_second, payload):
    tiles = own.shape[0]
    core = lax.axis_index("patch") % 2

    def sides(low, high):
        (down, from_low), (up, from_high) = low, high

        @pl.when(core == 0)
        def _():
            payload[0:2] = up[2:4]
            payload[2:4] = from_high[2:4]

        @pl.when(core == 1)
        def _():
            payload[0:2] = from_low[2:4]
            payload[2:4] = down[2:4]

        for o in range(2):
            for s in range(2):
                tile = send[0, 1 + o, s]
                value = own[jnp.minimum(tile, tiles - 1)]
                for back in range(2):
                    value = value + jnp.where(
                        send[0, 0, back] == tile, from_low[back].astype(F32), 0.0
                    )
                    value = value + jnp.where(
                        send[0, 3, back] == tile, from_high[back].astype(F32), 0.0
                    )
                payload[4 + 2 * o + s] = value.astype(BF16)
                payload[8, 16 * (2 * o + s) : 16 * (2 * o + s) + 16, :] = jnp.full(
                    (16, payload.shape[2]), tile.astype(F32)
                ).astype(BF16)

    by_chip(sides, (first, from_first), (second, from_second))


def gather_kernel(send, own, from_first, from_second, total):
    total[...] = own[...]

    def sides(from_low, from_high):
        for s in range(2):
            add_to(total, send[0, 0, s], from_low[s])
            add_to(total, send[0, 3, s], from_high[s])

    by_chip(sides, from_first, from_second)


def complete_kernel(send, partial, payload, arrived, smooth, second, first, total):
    tiles = partial.shape[0]
    total[...] = partial[...]
    for o in range(2):
        for s in range(2):
            add_to(total, send[0, 1 + o, s], arrived[2 * o + s])
    smooth[...] = total[...].astype(BF16)

    def sides(down, up):
        for s in range(2):
            down[s] = smooth[jnp.minimum(send[0, 0, s], tiles - 1)]
            up[s] = smooth[jnp.minimum(send[0, 3, s], tiles - 1)]
        marks = [arrived[8, 16 * i : 16 * i + 1, :].astype(F32) for i in range(4)]
        for o in range(2):
            out = (down, up)[o]
            for s in range(2):
                mine = 2 * o + s
                tile = arrived[4 + mine].astype(F32) + payload[mine].astype(F32)
                for other in range(2):
                    theirs = 2 * (1 - o) + other
                    tile = tile + jnp.where(
                        marks[mine] == marks[theirs], payload[theirs].astype(F32), 0.0
                    )
                out[2 + s] = tile.astype(BF16)

    by_chip(sides, first, second)


def forward_kernel(
    pattern, smooth, first, second, from_first, from_second, interp, conv, out, entries
):
    tiles, tile_len, fine = interp.shape
    count = conv.shape[1]
    members, level_len, _ = out.shape
    core = lax.axis_index("patch") % 2
    entries[0:tiles] = smooth[...]

    def sides(low, high):
        (down, from_low), (up, from_high) = low, high
        entries[tiles : tiles + 2] = from_high[0:2]
        entries[tiles + 6 : tiles + 8] = from_low[0:2]

        @pl.when(core == 0)
        def _():
            entries[tiles + 2 : tiles + 4] = down[2:4]
            entries[tiles + 4 : tiles + 6] = from_low[2:4]

        @pl.when(core == 1)
        def _():
            entries[tiles + 2 : tiles + 4] = from_high[2:4]
            entries[tiles + 4 : tiles + 6] = up[2:4]

    by_chip(sides, (first, from_first), (second, from_second))
    for t in range(tiles):
        picked = jnp.concatenate([entries[pattern[t, k]] for k in range(count)], axis=1)
        mixed = nn(picked, conv[t].reshape(count * tile_len, tile_len)).astype(BF16)
        out[:, :, t * fine : (t + 1) * fine] = nn(mixed, interp[t]).reshape(
            members, level_len, fine
        )


VMEM = pl.BlockSpec(memory_space=pltpu.VMEM)
SMEM = pl.BlockSpec(memory_space=pltpu.SMEM)
HBM = pl.BlockSpec(memory_space=pltpu.HBM)


def in_hbm(array):
    return pltpu.with_memory_space_constraint(array, pltpu.HBM)


def call(kernel, outs, specs, ins, scratch=(), flops=1 << 24):
    return pl.pallas_call(
        kernel,
        out_shape=outs,
        in_specs=specs,
        out_specs=jax.tree.map(lambda _: VMEM, outs),
        scratch_shapes=list(scratch),
        compiler_params=pltpu.CompilerParams(vmem_limit_bytes=16 << 20),
        cost_estimate=pl.CostEstimate(flops=flops, bytes_accessed=1 << 20, transcendentals=0),
    )(*ins)


def shape(dims, dtype):
    return jax.ShapeDtypeStruct(dims, dtype)


def shards(fields, interp, conv_weight, vert_weight, send_tiles, tile_pattern):
    members, level_len, columns = fields.shape
    tiles, tile_len, fine = interp.shape
    halo = vert_weight.shape[1] - 1
    rows = members * level_len
    patches = lax.axis_size("patch")
    levs = lax.axis_size("lev")
    tile_shape = (rows, tile_len)
    tile_list = shape((tiles,) + tile_shape, F32)
    narrow_list = shape((tiles,) + tile_shape, BF16)
    edge_list = shape((tiles, members * halo, tile_len), BF16)
    four = shape((4,) + tile_shape, BF16)

    def swap(block, start):
        partner = [
            (i, (i + 2) % patches if (i - start) % 4 < 2 else (i - 2) % patches)
            for i in range(patches)
        ]
        return lax.ppermute(block, "patch", partner)

    coarse, top, bottom = call(
        functools.partial(restrict_kernel, halo),
        (narrow_list, edge_list, edge_list),
        [HBM, HBM],
        (in_hbm(fields), in_hbm(interp)),
        [
            pltpu.VMEM((tiles, members, level_len, fine), BF16),
            pltpu.VMEM((tiles, tile_len, fine), BF16),
            pltpu.SemaphoreType.DMA((2, tiles)),
        ],
    )
    low = lax.ppermute(top, "lev", [(i, i + 1) for i in range(levs - 1)])
    high = lax.ppermute(bottom, "lev", [(i + 1, i) for i in range(levs - 1)])
    partial, halo_matrix, pattern, conv = call(
        functools.partial(vertical_kernel, level_len, halo),
        (
            tile_list,
            shape((rows, 4 * members * halo), BF16),
            shape(tile_pattern.shape, jnp.int32),
            shape(conv_weight.shape, BF16),
        ),
        [VMEM] * 3 + [HBM],
        (coarse, vert_weight, tile_pattern, in_hbm(conv_weight)),
        [pltpu.SemaphoreType.DMA],
    )
    own, second, first = call(
        adjoint_kernel,
        (tile_list, four, four),
        [SMEM] + [VMEM] * 5,
        (pattern, partial, halo_matrix, low, high, conv),
        [pltpu.VMEM((tiles + 8,) + tile_shape, F32)],
    )
    from_second = swap(second, 2)
    from_first = swap(first, 0)
    payload = call(
        partner_kernel,
        shape((9,) + tile_shape, BF16),
        [SMEM] + [VMEM] * 5,
        (send_tiles, own, first, second, from_first, from_second),
    )
    arrived = lax.ppermute(payload, "patch", [(i, i ^ 1) for i in range(patches)])
    total = call(
        gather_kernel,
        tile_list,
        [SMEM] + [VMEM] * 3,
        (send_tiles, own, from_first, from_second),
    )
    smooth, second, first = call(
        complete_kernel,
        (narrow_list, four, four),
        [SMEM] + [VMEM] * 3,
        (send_tiles, total, payload, arrived),
        [pltpu.VMEM((tiles,) + tile_shape, F32)],
    )
    from_second = swap(second, 2)
    from_first = swap(first, 0)
    return call(
        forward_kernel,
        shape(fields.shape, F32),
        [SMEM] + [VMEM] * 7,
        (pattern, smooth, first, second, from_first, from_second, interp, conv),
        [pltpu.VMEM((tiles + 8,) + tile_shape, BF16)],
    )


def solution(mesh):
    in_specs = (
        P(None, "lev", "patch"),
        P("patch", None, None),
        P("patch", None, None, None),
        P(),
        P("patch", None, None),
        P("patch", None),
    )
    out_specs = P(None, "lev", "patch")
    return jax.shard_map(shards, mesh=mesh, in_specs=in_specs, out_specs=out_specs, check_vma=False)
```

```python
import functools

import jax
import jax.numpy as jnp
from jax import lax
from jax.experimental import pallas as pl
from jax.experimental.pallas import tpu as pltpu
from jax.sharding import PartitionSpec as P

BF16 = jnp.bfloat16
F32 = jnp.float32
HIGHEST = lax.Precision.HIGHEST


def nn(a, b):
    return lax.dot_general(a, b, (((1,), (0,)), ((), ())), preferred_element_type=F32)


def nt(a, b):
    return lax.dot_general(a, b, (((1,), (1,)), ((), ())), preferred_element_type=F32)


def iota(shape, dim):
    return lax.broadcasted_iota(jnp.int32, shape, dim)


def split(a):
    high = a.astype(BF16)
    return high, (a - high.astype(F32)).astype(BF16)


def restrict_kernel(
    halo, fields, interp, weights, pattern, coarse, top, bottom, weights_copy, pattern_copy,
    block, bases, sems
):
    tiles, tile_len, fine = bases.shape
    members, level_len, _ = block.shape
    rows = members * level_len
    pairs = ((interp, bases), (fields, block), (weights, weights_copy), (pattern, pattern_copy))
    copies = [
        pltpu.make_async_copy(source, target, sems.at[i])
        for i, (source, target) in enumerate(pairs)
    ]
    for copy in copies:
        copy.start()
    first_half = iota((members // 2, 2 * halo, tile_len), 1) < halo
    for copy in copies[:2]:
        copy.wait()
    for t in range(tiles):
        span = slice(t * fine, (t + 1) * fine)
        value = nt(block[:, :, span].reshape(rows, fine), bases[t])
        coarse[t] = value.astype(BF16)
        group = value.reshape(members // 2, 2, level_len, tile_len)
        even, odd = group[:, 0, : 2 * halo], group[:, 1, : 2 * halo]
        bottom[t] = (
            jnp.where(first_half, even, pltpu.roll(odd, halo, 1))
            .reshape(members * halo, tile_len)
            .astype(BF16)
        )
        even, odd = group[:, 0, level_len - 2 * halo :], group[:, 1, level_len - 2 * halo :]
        top[t] = (
            jnp.where(first_half, pltpu.roll(even, halo, 1), odd)
            .reshape(members * halo, tile_len)
            .astype(BF16)
        )
    for copy in copies[2:]:
        copy.wait()


def vertical_kernel(
    level_len, halo, coarse, weights, conv, partial, halo_matrix, conv_copy, sem
):
    fetch = pltpu.make_async_copy(conv, conv_copy, sem)
    fetch.start()
    tiles, rows, tile_len = coarse.shape
    halo_rows = rows // level_len * halo
    taps, levels = weights.shape
    half = taps // 2
    start = lax.axis_index("lev") * level_len
    distance = iota((levels, levels), 0) - iota((levels, levels), 1)
    table = weights[...]
    band = jnp.zeros((levels, levels), F32)
    for j in range(taps):
        band = band + jnp.where(distance == j - half, table[j : j + 1, :], 0.0)
    both = lax.dot_general(
        band, band, (((0,), (0,)), ((), ())), precision=HIGHEST, preferred_element_type=F32
    )
    pick = (
        iota((rows, levels), 1) == start + iota((rows, levels), 0) % level_len
    ).astype(BF16)
    place = iota((2 * halo_rows, levels), 0)
    level = jnp.where(
        place < halo_rows, start - halo + place % halo, start + level_len + place % halo
    )
    pick_halo = (iota((2 * halo_rows, levels), 1) == level).astype(BF16)
    same = iota((rows, rows), 0) // level_len == iota((rows, rows), 1) // level_len
    column = iota((rows, 2 * halo_rows), 1) % halo_rows
    same_halo = iota((rows, 2 * halo_rows), 0) // level_len == column // halo
    own_parts = []
    for i, part in enumerate(split(both)):
        chosen = nn(pick, part).astype(BF16)
        own_parts.append(jnp.where(same, nt(chosen, pick), 0.0).astype(BF16))
        halo_matrix[:, i * 2 * halo_rows : (i + 1) * 2 * halo_rows] = jnp.where(
            same_halo, nt(chosen, pick_halo), 0.0
        ).astype(BF16)
    own_matrix = jnp.concatenate(own_parts, axis=1)
    for t in range(tiles):
        value = coarse[t]
        partial[t] = nn(own_matrix, jnp.concatenate([value, value], axis=0))
    fetch.wait()


def by_chip(body, first, second):
    odd = lax.axis_index("patch") // 2 % 2

    @pl.when(odd == 0)
    def _():
        body(second, first)

    @pl.when(odd == 1)
    def _():
        body(first, second)


def adjoint_kernel(
    pattern, partial, halo_matrix, low, high, conv, own, second, first,
    smooth, products, entries, table, sem
):
    tiles, rows, tile_len = partial.shape
    count = conv.shape[1]
    fetch = pltpu.make_async_copy(pattern, table, sem)
    fetch.start()
    matrix = halo_matrix[...]
    for t in range(tiles):
        edge = jnp.concatenate([low[t], high[t]], axis=0)
        smooth[t] = (
            partial[t] + nn(matrix, jnp.concatenate([edge, edge], axis=0))
        ).astype(BF16)
    for t in range(tiles):
        products[t] = nt(smooth[t], conv[t].reshape(count * tile_len, tile_len))
    entries[...] = jnp.zeros_like(entries)
    fetch.wait()
    for t in range(tiles):
        for k in range(count):
            entry = table[t, k]
            entries[entry] += products[t, :, k * tile_len : (k + 1) * tile_len]
    own[...] = entries[:tiles]

    def sides(down, up):
        up[...] = entries[tiles : tiles + 4].astype(BF16)
        down[0:2] = entries[tiles + 6 : tiles + 8].astype(BF16)
        down[2:4] = entries[tiles + 4 : tiles + 6].astype(BF16)

    by_chip(sides, first, second)


def add_to(total, tile, piece):
    @pl.when(tile < total.shape[0])
    def _():
        total[tile] += piece.astype(F32)


def partner_kernel(send, own, second, first, from_second, from_first, payload):
    tiles = own.shape[0]
    core = lax.axis_index("patch") % 2

    def sides(low, high):
        (down, from_low), (up, from_high) = low, high

        @pl.when(core == 0)
        def _():
            payload[0:2] = up[2:4]
            payload[2:4] = from_high[2:4]

        @pl.when(core == 1)
        def _():
            payload[0:2] = from_low[2:4]
            payload[2:4] = down[2:4]

        for o in range(2):
            for s in range(2):
                tile = send[0, 1 + o, s]
                value = own[jnp.minimum(tile, tiles - 1)]
                for back in range(2):
                    value = value + jnp.where(
                        send[0, 0, back] == tile, from_low[back].astype(F32), 0.0
                    )
                    value = value + jnp.where(
                        send[0, 3, back] == tile, from_high[back].astype(F32), 0.0
                    )
                payload[4 + 2 * o + s] = value.astype(BF16)
                payload[8, 16 * (2 * o + s) : 16 * (2 * o + s) + 16, :] = jnp.full(
                    (16, payload.shape[2]), tile.astype(F32)
                ).astype(BF16)

    by_chip(sides, (first, from_first), (second, from_second))


def gather_kernel(send, own, from_second, from_first, total):
    total[...] = own[...]

    def sides(from_low, from_high):
        for s in range(2):
            add_to(total, send[0, 0, s], from_low[s])
            add_to(total, send[0, 3, s], from_high[s])

    by_chip(sides, from_first, from_second)


def complete_kernel(send, partial, payload, arrived, smooth, second, first, total):
    tiles = partial.shape[0]
    total[...] = partial[...]
    for o in range(2):
        for s in range(2):
            add_to(total, send[0, 1 + o, s], arrived[2 * o + s])
    smooth[...] = total[...].astype(BF16)

    def sides(down, up):
        for s in range(2):
            down[s] = smooth[jnp.minimum(send[0, 0, s], tiles - 1)]
            up[s] = smooth[jnp.minimum(send[0, 3, s], tiles - 1)]
        marks = [arrived[8, 16 * i : 16 * i + 1, :].astype(F32) for i in range(4)]
        for o in range(2):
            out = (down, up)[o]
            for s in range(2):
                mine = 2 * o + s
                tile = arrived[4 + mine].astype(F32) + payload[mine].astype(F32)
                for other in range(2):
                    theirs = 2 * (1 - o) + other
                    tile = tile + jnp.where(
                        marks[mine] == marks[theirs], payload[theirs].astype(F32), 0.0
                    )
                out[2 + s] = tile.astype(BF16)

    by_chip(sides, first, second)


def forward_kernel(
    pattern, smooth, second, first, from_second, from_first, interp, conv, out,
    entries, mixed, table, sem
):
    tiles, tile_len, fine = interp.shape
    count = conv.shape[1]
    members, level_len, _ = out.shape
    core = lax.axis_index("patch") % 2
    fetch = pltpu.make_async_copy(pattern, table, sem)
    fetch.start()
    entries[0:tiles] = smooth[...]

    def sides(low, high):
        (down, from_low), (up, from_high) = low, high
        entries[tiles : tiles + 2] = from_high[0:2]
        entries[tiles + 6 : tiles + 8] = from_low[0:2]

        @pl.when(core == 0)
        def _():
            entries[tiles + 2 : tiles + 4] = down[2:4]
            entries[tiles + 4 : tiles + 6] = from_low[2:4]

        @pl.when(core == 1)
        def _():
            entries[tiles + 2 : tiles + 4] = from_high[2:4]
            entries[tiles + 4 : tiles + 6] = up[2:4]

    by_chip(sides, (first, from_first), (second, from_second))
    fetch.wait()
    for t in range(tiles):
        picked = jnp.concatenate([entries[table[t, k]] for k in range(count)], axis=1)
        mixed[t] = nn(picked, conv[t].reshape(count * tile_len, tile_len)).astype(BF16)
    for t in range(tiles):
        out[:, :, t * fine : (t + 1) * fine] = nn(mixed[t], interp[t]).reshape(
            members, level_len, fine
        )


VMEM = pl.BlockSpec(memory_space=pltpu.VMEM)
SMEM = pl.BlockSpec(memory_space=pltpu.SMEM)
HBM = pl.BlockSpec(memory_space=pltpu.HBM)


def in_hbm(array):
    return pltpu.with_memory_space_constraint(array, pltpu.HBM)


def call(kernel, outs, specs, ins, scratch=(), flops=1 << 24):
    return pl.pallas_call(
        kernel,
        out_shape=outs,
        in_specs=specs,
        out_specs=jax.tree.map(lambda _: VMEM, outs),
        scratch_shapes=list(scratch),
        compiler_params=pltpu.CompilerParams(vmem_limit_bytes=16 << 20),
        cost_estimate=pl.CostEstimate(flops=flops, bytes_accessed=1 << 20, transcendentals=0),
    )(*ins)


def shape(dims, dtype):
    return jax.ShapeDtypeStruct(dims, dtype)


def shards(fields, interp, conv_weight, vert_weight, send_tiles, tile_pattern):
    members, level_len, columns = fields.shape
    tiles, tile_len, fine = interp.shape
    halo = vert_weight.shape[1] - 1
    rows = members * level_len
    patches = lax.axis_size("patch")
    levs = lax.axis_size("lev")
    tile_shape = (rows, tile_len)
    tile_list = shape((tiles,) + tile_shape, F32)
    narrow_list = shape((tiles,) + tile_shape, BF16)
    edge_list = shape((tiles, members * halo, tile_len), BF16)
    four = shape((4,) + tile_shape, BF16)

    def swap(block, start):
        partner = [
            (i, (i + 2) % patches if (i - start) % 4 < 2 else (i - 2) % patches)
            for i in range(patches)
        ]
        return lax.ppermute(block, "patch", partner)

    table = pltpu.SMEM(tile_pattern.shape, jnp.int32)
    coarse, top, bottom, weights, pattern = call(
        functools.partial(restrict_kernel, halo),
        (
            narrow_list,
            edge_list,
            edge_list,
            shape(vert_weight.shape[::-1], F32),
            shape(tile_pattern.shape, jnp.int32),
        ),
        [HBM] * 4,
        [in_hbm(array) for array in (fields, interp, vert_weight.T, tile_pattern)],
        [
            pltpu.VMEM(fields.shape, BF16),
            pltpu.VMEM((tiles, tile_len, fine), BF16),
            pltpu.SemaphoreType.DMA((4,)),
        ],
    )
    low = lax.ppermute(top, "lev", [(i, i + 1) for i in range(levs - 1)])
    high = lax.ppermute(bottom, "lev", [(i + 1, i) for i in range(levs - 1)])
    partial, halo_matrix, conv = call(
        functools.partial(vertical_kernel, level_len, halo),
        (
            tile_list,
            shape((rows, 4 * members * halo), BF16),
            shape(conv_weight.shape, BF16),
        ),
        [VMEM] * 2 + [HBM],
        (coarse, weights, in_hbm(conv_weight)),
        [pltpu.SemaphoreType.DMA],
    )
    own, second, first = call(
        adjoint_kernel,
        (tile_list, four, four),
        [VMEM] * 6,
        (pattern, partial, halo_matrix, low, high, conv),
        [
            pltpu.VMEM((tiles,) + tile_shape, BF16),
            pltpu.VMEM((tiles, rows, conv_weight.shape[1] * tile_len), F32),
            pltpu.VMEM((tiles + 8,) + tile_shape, F32),
            table,
            pltpu.SemaphoreType.DMA,
        ],
    )
    from_second = swap(second, 2)
    from_first = swap(first, 0)
    payload = call(
        partner_kernel,
        shape((9,) + tile_shape, BF16),
        [SMEM] + [VMEM] * 5,
        (send_tiles, own, second, first, from_second, from_first),
    )
    arrived = lax.ppermute(payload, "patch", [(i, i ^ 1) for i in range(patches)])
    total = call(
        gather_kernel,
        tile_list,
        [SMEM] + [VMEM] * 3,
        (send_tiles, own, from_second, from_first),
    )
    smooth, second, first = call(
        complete_kernel,
        (narrow_list, four, four),
        [SMEM] + [VMEM] * 3,
        (send_tiles, total, payload, arrived),
        [pltpu.VMEM((tiles,) + tile_shape, F32)],
    )
    from_second = swap(second, 2)
    from_first = swap(first, 0)
    return call(
        forward_kernel,
        shape(fields.shape, F32),
        [VMEM] * 8,
        (pattern, smooth, second, first, from_second, from_first, interp, conv),
        [
            pltpu.VMEM((tiles + 8,) + tile_shape, BF16),
            pltpu.VMEM((tiles,) + tile_shape, BF16),
            table,
            pltpu.SemaphoreType.DMA,
        ],
    )


def solution(mesh):
    in_specs = (
        P(None, "lev", "patch"),
        P("patch", None, None),
        P("patch", None, None, None),
        P(),
        P("patch", None, None),
        P("patch", None),
    )
    out_specs = P(None, "lev", "patch")
    return jax.shard_map(shards, mesh=mesh, in_specs=in_specs, out_specs=out_specs, check_vma=False)
```

```python
import functools

import jax
import jax.numpy as jnp
from jax import lax
from jax.experimental import pallas as pl
from jax.experimental.pallas import tpu as pltpu
from jax.sharding import PartitionSpec as P

BF16 = jnp.bfloat16
F32 = jnp.float32
HIGHEST = lax.Precision.HIGHEST


def nn(a, b):
    return lax.dot_general(a, b, (((1,), (0,)), ((), ())), preferred_element_type=F32)


def nt(a, b):
    return lax.dot_general(a, b, (((1,), (1,)), ((), ())), preferred_element_type=F32)


def iota(shape, dim):
    return lax.broadcasted_iota(jnp.int32, shape, dim)


def split(a):
    high = a.astype(BF16)
    return high, (a - high.astype(F32)).astype(BF16)


def restrict_kernel(
    halo, fields, interp, weights, pattern, coarse, top, bottom, weights_copy, pattern_copy,
    block, bases, sems
):
    tiles, tile_len, fine = bases.shape
    members, level_len, _ = block.shape
    rows = members * level_len
    pairs = ((interp, bases), (fields, block), (weights, weights_copy), (pattern, pattern_copy))
    copies = [
        pltpu.make_async_copy(source, target, sems.at[i])
        for i, (source, target) in enumerate(pairs)
    ]
    for copy in copies:
        copy.start()
    first_half = iota((members // 2, 2 * halo, tile_len), 1) < halo
    for copy in copies[:2]:
        copy.wait()
    for t in range(tiles):
        span = slice(t * fine, (t + 1) * fine)
        value = nt(block[:, :, span].reshape(rows, fine), bases[t])
        coarse[t] = value.astype(BF16)
        group = value.reshape(members // 2, 2, level_len, tile_len)
        even, odd = group[:, 0, : 2 * halo], group[:, 1, : 2 * halo]
        bottom[t] = (
            jnp.where(first_half, even, pltpu.roll(odd, halo, 1))
            .reshape(members * halo, tile_len)
            .astype(BF16)
        )
        even, odd = group[:, 0, level_len - 2 * halo :], group[:, 1, level_len - 2 * halo :]
        top[t] = (
            jnp.where(first_half, pltpu.roll(even, halo, 1), odd)
            .reshape(members * halo, tile_len)
            .astype(BF16)
        )
    for copy in copies[2:]:
        copy.wait()


def vertical_kernel(
    level_len, halo, coarse, weights, conv, partial, halo_matrix, conv_copy, sem
):
    fetch = pltpu.make_async_copy(conv, conv_copy, sem)
    fetch.start()
    tiles, rows, tile_len = coarse.shape
    halo_rows = rows // level_len * halo
    taps, levels = weights.shape
    half = taps // 2
    start = lax.axis_index("lev") * level_len
    distance = iota((levels, levels), 0) - iota((levels, levels), 1)
    table = weights[...]
    band = jnp.zeros((levels, levels), F32)
    for j in range(taps):
        band = band + jnp.where(distance == j - half, table[j : j + 1, :], 0.0)
    both = lax.dot_general(
        band, band, (((0,), (0,)), ((), ())), precision=HIGHEST, preferred_element_type=F32
    )
    pick = (
        iota((rows, levels), 1) == start + iota((rows, levels), 0) % level_len
    ).astype(BF16)
    place = iota((2 * halo_rows, levels), 0)
    level = jnp.where(
        place < halo_rows, start - halo + place % halo, start + level_len + place % halo
    )
    pick_halo = (iota((2 * halo_rows, levels), 1) == level).astype(BF16)
    same = iota((rows, rows), 0) // level_len == iota((rows, rows), 1) // level_len
    column = iota((rows, 2 * halo_rows), 1) % halo_rows
    same_halo = iota((rows, 2 * halo_rows), 0) // level_len == column // halo
    own_parts = []
    for i, part in enumerate(split(both)):
        chosen = nn(pick, part).astype(BF16)
        own_parts.append(jnp.where(same, nt(chosen, pick), 0.0).astype(BF16))
        halo_matrix[:, i * 2 * halo_rows : (i + 1) * 2 * halo_rows] = jnp.where(
            same_halo, nt(chosen, pick_halo), 0.0
        ).astype(BF16)
    own_matrix = jnp.concatenate(own_parts, axis=1)
    for t in range(tiles):
        value = coarse[t]
        partial[t] = nn(own_matrix, jnp.concatenate([value, value], axis=0))
    fetch.wait()


def by_chip(body, first, second):
    odd = lax.axis_index("patch") // 2 % 2

    @pl.when(odd == 0)
    def _():
        body(second, first)

    @pl.when(odd == 1)
    def _():
        body(first, second)


def find_terms(table, place, tiles):
    _, count = table.shape
    for i in range(place.shape[0]):
        place[i] = tiles * count
    for t in range(tiles):
        for k in range(count):
            place[table[t, k] * tiles + t] = t * count + k


def form_products(smooth, conv, products):
    tiles, count, tile_len, _ = conv.shape
    products[tiles * count] = jnp.zeros(products.shape[1:], F32)
    for t in range(tiles):
        value = nt(smooth[t], conv[t].reshape(count * tile_len, tile_len))
        for k in range(count):
            products[t * count + k] = value[:, k * tile_len : (k + 1) * tile_len]


def entry_sum(products, place, entry, tiles):
    terms = [products[place[entry * tiles + t]] for t in range(tiles)]
    while len(terms) > 1:
        terms = [terms[i] + terms[i + 1] for i in range(0, len(terms), 2)]
    return terms[0]


def adjoint_kernel(
    pattern, partial, halo_matrix, low, high, conv, smooth, second, first,
    products, table, place, sem
):
    tiles = partial.shape[0]
    fetch = pltpu.make_async_copy(pattern, table, sem)
    fetch.start()
    matrix = halo_matrix[...]
    for t in range(tiles):
        edge = jnp.concatenate([low[t], high[t]], axis=0)
        smooth[t] = (
            partial[t] + nn(matrix, jnp.concatenate([edge, edge], axis=0))
        ).astype(BF16)
    form_products(smooth, conv, products)
    fetch.wait()
    find_terms(table, place, tiles)

    def sides(down, up):
        for i in range(4):
            up[i] = entry_sum(products, place, tiles + i, tiles).astype(BF16)
            down[i] = entry_sum(products, place, tiles + 4 + (i + 2) % 4, tiles).astype(BF16)

    by_chip(sides, first, second)


def own_kernel(pattern, smooth, conv, own, products, table, place, sem):
    tiles = own.shape[0]
    fetch = pltpu.make_async_copy(pattern, table, sem)
    fetch.start()
    form_products(smooth, conv, products)
    fetch.wait()
    find_terms(table, place, tiles)
    for t in range(tiles):
        own[t] = entry_sum(products, place, t, tiles)


def add_to(total, tile, piece):
    last = total.shape[0] - 1
    total[jnp.minimum(tile, last)] += jnp.where(tile <= last, piece.astype(F32), 0.0)


def partner_kernel(send, own, second, first, from_second, from_first, payload, table, sem):
    tiles = own.shape[0]
    core = lax.axis_index("patch") % 2
    fetch = pltpu.make_async_copy(send, table, sem)
    fetch.start()

    def copies(low, high):
        (down, from_low), (up, from_high) = low, high

        @pl.when(core == 0)
        def _():
            payload[0:2] = up[2:4]
            payload[2:4] = from_high[2:4]

        @pl.when(core == 1)
        def _():
            payload[0:2] = from_low[2:4]
            payload[2:4] = down[2:4]

    by_chip(copies, (first, from_first), (second, from_second))
    fetch.wait()
    for i in range(4):
        tile = table[0, 1 + i // 2, i % 2]
        payload[8, 16 * i : 16 * i + 16, :] = jnp.full(
            (16, payload.shape[2]), tile.astype(F32)
        ).astype(BF16)

    def sums(from_low, from_high):
        for i in range(4):
            tile = table[0, 1 + i // 2, i % 2]
            value = own[jnp.minimum(tile, tiles - 1)]
            for back in range(2):
                for link, source in ((0, from_low), (3, from_high)):
                    value = value + jnp.where(
                        table[0, link, back] == tile, source[back].astype(F32), 0.0
                    )
            payload[4 + i] = value.astype(BF16)

    by_chip(sums, from_first, from_second)


def gather_kernel(send, own, from_second, from_first, total):
    total[...] = own[...]

    def sides(from_low, from_high):
        for s in range(2):
            add_to(total, send[0, 0, s], from_low[s])
            add_to(total, send[0, 3, s], from_high[s])

    by_chip(sides, from_first, from_second)


def complete_kernel(
    send, partial, payload, arrived, smooth, second, first, total, table, sem
):
    tiles = partial.shape[0]
    fetch = pltpu.make_async_copy(send, table, sem)
    fetch.start()
    total[...] = partial[...]
    marks = [arrived[8, 16 * i : 16 * i + 1, :].astype(F32) for i in range(4)]
    pieces = [payload[i].astype(F32) for i in range(4)]
    theirs = []
    for i in range(4):
        tile = arrived[4 + i].astype(F32) + pieces[i]
        for j in (2, 3) if i < 2 else (0, 1):
            tile = tile + jnp.where(marks[i] == marks[j], pieces[j], 0.0)
        theirs.append(tile.astype(BF16))

    def forwarded(down, up):
        for s in range(2):
            down[2 + s] = theirs[s]
            up[2 + s] = theirs[2 + s]

    by_chip(forwarded, first, second)
    fetch.wait()
    for i in range(4):
        add_to(total, table[0, 1 + i // 2, i % 2], arrived[i])
    smooth[...] = total[...].astype(BF16)

    def sides(down, up):
        for s in range(2):
            down[s] = smooth[jnp.minimum(table[0, 0, s], tiles - 1)]
            up[s] = smooth[jnp.minimum(table[0, 3, s], tiles - 1)]

    by_chip(sides, first, second)


def forward_kernel(
    pattern, smooth, second, first, from_second, from_first, interp, conv, out,
    entries, mixed, table, sem
):
    tiles, tile_len, fine = interp.shape
    count = conv.shape[1]
    members, level_len, _ = out.shape
    core = lax.axis_index("patch") % 2
    fetch = pltpu.make_async_copy(pattern, table, sem)
    fetch.start()
    entries[0:tiles] = smooth[...]

    def sides(low, high):
        (down, from_low), (up, from_high) = low, high
        entries[tiles : tiles + 2] = from_high[0:2]
        entries[tiles + 6 : tiles + 8] = from_low[0:2]

        @pl.when(core == 0)
        def _():
            entries[tiles + 2 : tiles + 4] = down[2:4]
            entries[tiles + 4 : tiles + 6] = from_low[2:4]

        @pl.when(core == 1)
        def _():
            entries[tiles + 2 : tiles + 4] = from_high[2:4]
            entries[tiles + 4 : tiles + 6] = up[2:4]

    by_chip(sides, (first, from_first), (second, from_second))
    fetch.wait()
    for t in range(tiles):
        picked = jnp.concatenate([entries[table[t, k]] for k in range(count)], axis=1)
        mixed[t] = nn(picked, conv[t].reshape(count * tile_len, tile_len)).astype(BF16)
    for t in range(tiles):
        out[:, :, t * fine : (t + 1) * fine] = nn(mixed[t], interp[t]).reshape(
            members, level_len, fine
        )


VMEM = pl.BlockSpec(memory_space=pltpu.VMEM)
SMEM = pl.BlockSpec(memory_space=pltpu.SMEM)
HBM = pl.BlockSpec(memory_space=pltpu.HBM)


def in_hbm(array):
    return pltpu.with_memory_space_constraint(array, pltpu.HBM)


def call(kernel, outs, specs, ins, scratch=(), flops=1 << 24):
    return pl.pallas_call(
        kernel,
        out_shape=outs,
        in_specs=specs,
        out_specs=jax.tree.map(lambda _: VMEM, outs),
        scratch_shapes=list(scratch),
        compiler_params=pltpu.CompilerParams(vmem_limit_bytes=16 << 20),
        cost_estimate=pl.CostEstimate(flops=flops, bytes_accessed=1 << 20, transcendentals=0),
    )(*ins)


def shape(dims, dtype):
    return jax.ShapeDtypeStruct(dims, dtype)


def shards(fields, interp, conv_weight, vert_weight, send_tiles, tile_pattern):
    members, level_len, columns = fields.shape
    tiles, tile_len, fine = interp.shape
    halo = vert_weight.shape[1] - 1
    rows = members * level_len
    patches = lax.axis_size("patch")
    levs = lax.axis_size("lev")
    tile_shape = (rows, tile_len)
    tile_list = shape((tiles,) + tile_shape, F32)
    narrow_list = shape((tiles,) + tile_shape, BF16)
    edge_list = shape((tiles, members * halo, tile_len), BF16)
    four = shape((4,) + tile_shape, BF16)

    def swap(block, start):
        partner = [
            (i, (i + 2) % patches if (i - start) % 4 < 2 else (i - 2) % patches)
            for i in range(patches)
        ]
        return lax.ppermute(block, "patch", partner)

    table = pltpu.SMEM(tile_pattern.shape, jnp.int32)
    coarse, top, bottom, weights, pattern = call(
        functools.partial(restrict_kernel, halo),
        (
            narrow_list,
            edge_list,
            edge_list,
            shape(vert_weight.shape[::-1], F32),
            shape(tile_pattern.shape, jnp.int32),
        ),
        [HBM] * 4,
        [in_hbm(array) for array in (fields, interp, vert_weight.T, tile_pattern)],
        [
            pltpu.VMEM(fields.shape, BF16),
            pltpu.VMEM((tiles, tile_len, fine), BF16),
            pltpu.SemaphoreType.DMA((4,)),
        ],
    )
    low = lax.ppermute(top, "lev", [(i, i + 1) for i in range(levs - 1)])
    high = lax.ppermute(bottom, "lev", [(i + 1, i) for i in range(levs - 1)])
    partial, halo_matrix, conv = call(
        functools.partial(vertical_kernel, level_len, halo),
        (
            tile_list,
            shape((rows, 4 * members * halo), BF16),
            shape(conv_weight.shape, BF16),
        ),
        [VMEM] * 2 + [HBM],
        (coarse, weights, in_hbm(conv_weight)),
        [pltpu.SemaphoreType.DMA],
    )
    place = pltpu.SMEM((2 * tiles * tiles,), jnp.int32)
    sem = pltpu.SemaphoreType.DMA
    count = conv_weight.shape[1]
    products = pltpu.VMEM((tiles * count + 1,) + tile_shape, F32)
    vertical, second, first = call(
        adjoint_kernel,
        (narrow_list, four, four),
        [VMEM] * 6,
        (pattern, partial, halo_matrix, low, high, conv),
        [products, table, place, sem],
    )
    from_second = swap(second, 2)
    from_first = swap(first, 0)
    own = call(
        own_kernel,
        tile_list,
        [VMEM] * 3,
        (pattern, vertical, conv),
        [products, table, place, sem],
    )
    links = pltpu.SMEM(send_tiles.shape, jnp.int32)
    payload = call(
        partner_kernel,
        shape((9,) + tile_shape, BF16),
        [VMEM] * 6,
        (send_tiles, own, second, first, from_second, from_first),
        [links, sem],
    )
    arrived = lax.ppermute(payload, "patch", [(i, i ^ 1) for i in range(patches)])
    total = call(
        gather_kernel,
        tile_list,
        [SMEM] + [VMEM] * 3,
        (send_tiles, own, from_second, from_first),
    )
    smooth, second, first = call(
        complete_kernel,
        (narrow_list, four, four),
        [VMEM] * 4,
        (send_tiles, total, payload, arrived),
        [pltpu.VMEM((tiles,) + tile_shape, F32), links, sem],
    )
    from_second = swap(second, 2)
    from_first = swap(first, 0)
    return call(
        forward_kernel,
        shape(fields.shape, F32),
        [VMEM] * 8,
        (pattern, smooth, second, first, from_second, from_first, interp, conv),
        [
            pltpu.VMEM((tiles + 8,) + tile_shape, BF16),
            pltpu.VMEM((tiles,) + tile_shape, BF16),
            table,
            pltpu.SemaphoreType.DMA,
        ],
    )


def solution(mesh):
    in_specs = (
        P(None, "lev", "patch"),
        P("patch", None, None),
        P("patch", None, None, None),
        P(),
        P("patch", None, None),
        P("patch", None),
    )
    out_specs = P(None, "lev", "patch")
    return jax.shard_map(shards, mesh=mesh, in_specs=in_specs, out_specs=out_specs, check_vma=False)
```

```python
import functools

import jax
import jax.numpy as jnp
from jax import lax
from jax.experimental import pallas as pl
from jax.experimental.pallas import tpu as pltpu
from jax.sharding import PartitionSpec as P

BF16 = jnp.bfloat16
F32 = jnp.float32
HIGHEST = lax.Precision.HIGHEST


def nn(a, b):
    return lax.dot_general(a, b, (((1,), (0,)), ((), ())), preferred_element_type=F32)


def nt(a, b):
    return lax.dot_general(a, b, (((1,), (1,)), ((), ())), preferred_element_type=F32)


def lanes(t, width):
    return slice(t * width, (t + 1) * width)


def iota(shape, dim):
    return lax.broadcasted_iota(jnp.int32, shape, dim)


def split(a):
    high = a.astype(BF16)
    return high, (a - high.astype(F32)).astype(BF16)


def restrict_kernel(
    halo, fields, interp, weights, coarse, top, bottom, weights_copy,
    block, bases, sems
):
    tiles, tile_len, fine = bases.shape
    members, level_len, _ = block.shape
    rows = members * level_len
    pairs = ((interp, bases), (fields, block), (weights, weights_copy))
    copies = [
        pltpu.make_async_copy(source, target, sems.at[i])
        for i, (source, target) in enumerate(pairs)
    ]
    for copy in copies:
        copy.start()
    first_half = iota((members // 2, 2 * halo, tile_len), 1) < halo
    for copy in copies[:2]:
        copy.wait()
    for t in range(tiles):
        span = slice(t * fine, (t + 1) * fine)
        value = nt(block[:, :, span].reshape(rows, fine), bases[t])
        coarse[:, lanes(t, tile_len)] = value.astype(BF16)
        group = value.reshape(members // 2, 2, level_len, tile_len)
        even, odd = group[:, 0, : 2 * halo], group[:, 1, : 2 * halo]
        bottom[:, lanes(t, tile_len)] = (
            jnp.where(first_half, even, pltpu.roll(odd, halo, 1))
            .reshape(members * halo, tile_len)
            .astype(BF16)
        )
        even, odd = group[:, 0, level_len - 2 * halo :], group[:, 1, level_len - 2 * halo :]
        top[:, lanes(t, tile_len)] = (
            jnp.where(first_half, pltpu.roll(even, halo, 1), odd)
            .reshape(members * halo, tile_len)
            .astype(BF16)
        )
    for copy in copies[2:]:
        copy.wait()


def vertical_kernel(
    level_len, halo, coarse, weights, pattern, conv, partial, halo_matrix, own_blocks,
    received_blocks, conv_copy, table, sems
):
    fetches = (
        pltpu.make_async_copy(pattern, table, sems.at[0]),
        pltpu.make_async_copy(conv, conv_copy, sems.at[1]),
    )
    for fetch in fetches:
        fetch.start()
    tiles, count, tile_len, _ = conv.shape
    rows = coarse.shape[0]
    halo_rows = rows // level_len * halo
    taps, levels = weights.shape
    half = taps // 2
    start = lax.axis_index("lev") * level_len
    distance = iota((levels, levels), 0) - iota((levels, levels), 1)
    taken = weights[...]
    band = jnp.zeros((levels, levels), F32)
    for j in range(taps):
        band = band + jnp.where(distance == j - half, taken[j : j + 1, :], 0.0)
    both = lax.dot_general(
        band, band, (((0,), (0,)), ((), ())), precision=HIGHEST, preferred_element_type=F32
    )
    pick = (
        iota((rows, levels), 1) == start + iota((rows, levels), 0) % level_len
    ).astype(BF16)
    place = iota((2 * halo_rows, levels), 0)
    level = jnp.where(
        place < halo_rows, start - halo + place % halo, start + level_len + place % halo
    )
    pick_halo = (iota((2 * halo_rows, levels), 1) == level).astype(BF16)
    same = iota((rows, rows), 0) // level_len == iota((rows, rows), 1) // level_len
    column = iota((rows, 2 * halo_rows), 1) % halo_rows
    same_halo = iota((rows, 2 * halo_rows), 0) // level_len == column // halo
    own_parts = []
    for i, part in enumerate(split(both)):
        chosen = nn(pick, part).astype(BF16)
        own_parts.append(jnp.where(same, nt(chosen, pick), 0.0).astype(BF16))
        halo_matrix[:, i * 2 * halo_rows : (i + 1) * 2 * halo_rows] = jnp.where(
            same_halo, nt(chosen, pick_halo), 0.0
        ).astype(BF16)
    own_matrix = jnp.concatenate(own_parts, axis=1)
    value = coarse[...]
    partial[...] = nn(own_matrix, jnp.concatenate([value, value], axis=0))
    own_blocks[...] = jnp.zeros_like(own_blocks)
    received_blocks[...] = jnp.zeros_like(received_blocks)
    for fetch in fetches:
        fetch.wait()
    for t in range(tiles):
        for k in range(count):
            entry = table[t, k]

            @pl.when(entry < tiles)
            def _():
                own_blocks[entry, :, lanes(t, tile_len)] = conv_copy[t, k]

            @pl.when(entry >= tiles)
            def _():
                received_blocks[entry - tiles, :, lanes(t, tile_len)] = conv_copy[t, k]


def by_chip(body, first, second):
    odd = lax.axis_index("patch") // 2 % 2

    @pl.when(odd == 0)
    def _():
        body(second, first)

    @pl.when(odd == 1)
    def _():
        body(first, second)


def flat(blocks):
    return blocks[...].reshape(-1, blocks.shape[-1])


def adjoint_kernel(partial, halo_matrix, low, high, received_blocks, smooth, second, first):
    tile_len = received_blocks.shape[1]
    edge = jnp.concatenate([low[...], high[...]], axis=0)
    value = (
        partial[...] + nn(halo_matrix[...], jnp.concatenate([edge, edge], axis=0))
    ).astype(BF16)
    smooth[...] = value
    returning = nt(value, flat(received_blocks)).astype(BF16)

    def sides(down, up):
        for i in range(4):
            up[i] = returning[:, lanes(i, tile_len)]
            down[i] = returning[:, lanes(4 + (i + 2) % 4, tile_len)]

    by_chip(sides, first, second)


def own_kernel(smooth, own_blocks, own):
    value = nt(smooth[...], flat(own_blocks))
    for t in range(own.shape[0]):
        own[t] = value[:, lanes(t, own.shape[2])]


def add_to(total, tile, piece):
    last = total.shape[0] - 1
    total[jnp.minimum(tile, last)] += jnp.where(tile <= last, piece.astype(F32), 0.0)


def partner_kernel(send, own, second, first, from_second, from_first, payload, table, sem):
    tiles = own.shape[0]
    core = lax.axis_index("patch") % 2
    fetch = pltpu.make_async_copy(send, table, sem)
    fetch.start()

    def copies(low, high):
        (down, from_low), (up, from_high) = low, high

        @pl.when(core == 0)
        def _():
            payload[0:2] = up[2:4]
            payload[2:4] = from_high[2:4]

        @pl.when(core == 1)
        def _():
            payload[0:2] = from_low[2:4]
            payload[2:4] = down[2:4]

    by_chip(copies, (first, from_first), (second, from_second))
    fetch.wait()
    for i in range(4):
        tile = table[0, 1 + i // 2, i % 2]
        payload[8, 16 * i : 16 * i + 16, :] = jnp.full(
            (16, payload.shape[2]), tile.astype(F32)
        ).astype(BF16)

    def sums(from_low, from_high):
        for i in range(4):
            tile = table[0, 1 + i // 2, i % 2]
            value = own[jnp.minimum(tile, tiles - 1)]
            for back in range(2):
                for link, source in ((0, from_low), (3, from_high)):
                    value = value + jnp.where(
                        table[0, link, back] == tile, source[back].astype(F32), 0.0
                    )
            payload[4 + i] = value.astype(BF16)

    by_chip(sums, from_first, from_second)


def gather_kernel(send, own, from_second, from_first, total):
    total[...] = own[...]

    def sides(from_low, from_high):
        for s in range(2):
            add_to(total, send[0, 0, s], from_low[s])
            add_to(total, send[0, 3, s], from_high[s])

    by_chip(sides, from_first, from_second)


def complete_kernel(
    send, partial, payload, arrived, smooth, second, first, total, table, sem
):
    tiles = partial.shape[0]
    fetch = pltpu.make_async_copy(send, table, sem)
    fetch.start()
    total[...] = partial[...]
    marks = [arrived[8, 16 * i : 16 * i + 1, :].astype(F32) for i in range(4)]
    pieces = [payload[i].astype(F32) for i in range(4)]
    theirs = []
    for i in range(4):
        tile = arrived[4 + i].astype(F32) + pieces[i]
        for j in (2, 3) if i < 2 else (0, 1):
            tile = tile + jnp.where(marks[i] == marks[j], pieces[j], 0.0)
        theirs.append(tile.astype(BF16))

    def forwarded(down, up):
        for s in range(2):
            down[2 + s] = theirs[s]
            up[2 + s] = theirs[2 + s]

    by_chip(forwarded, first, second)
    fetch.wait()
    for i in range(4):
        add_to(total, table[0, 1 + i // 2, i % 2], arrived[i])
    smooth[...] = total[...].astype(BF16)

    def sides(down, up):
        for s in range(2):
            down[s] = smooth[jnp.minimum(table[0, 0, s], tiles - 1)]
            up[s] = smooth[jnp.minimum(table[0, 3, s], tiles - 1)]

    by_chip(sides, first, second)


def own_forward_kernel(smooth, own_blocks, partial):
    tiles = smooth.shape[0]
    picked = jnp.concatenate([smooth[t] for t in range(tiles)], axis=1)
    partial[...] = nn(picked, flat(own_blocks))


def forward_kernel(
    partial, second, first, from_second, from_first, received_blocks, interp, out, entries, mixed
):
    tiles, tile_len, fine = interp.shape
    members, level_len, _ = out.shape
    core = lax.axis_index("patch") % 2

    def put(place, source):
        for i in range(2):
            entries[:, lanes(place + i, tile_len)] = source[i]

    def sides(low, high):
        (down, from_low), (up, from_high) = low, high
        put(0, from_high.at[0:2])
        put(6, from_low.at[0:2])

        @pl.when(core == 0)
        def _():
            put(2, down.at[2:4])
            put(4, from_low.at[2:4])

        @pl.when(core == 1)
        def _():
            put(2, from_high.at[2:4])
            put(4, up.at[2:4])

    by_chip(sides, (first, from_first), (second, from_second))
    mixed[...] = (partial[...] + nn(entries[...], flat(received_blocks))).astype(BF16)
    for t in range(tiles):
        out[:, :, lanes(t, fine)] = nn(mixed[:, lanes(t, tile_len)], interp[t]).reshape(
            members, level_len, fine
        )


VMEM = pl.BlockSpec(memory_space=pltpu.VMEM)
SMEM = pl.BlockSpec(memory_space=pltpu.SMEM)
HBM = pl.BlockSpec(memory_space=pltpu.HBM)


def in_hbm(array):
    return pltpu.with_memory_space_constraint(array, pltpu.HBM)


def call(kernel, outs, specs, ins, scratch=(), flops=1 << 24):
    return pl.pallas_call(
        kernel,
        out_shape=outs,
        in_specs=specs,
        out_specs=jax.tree.map(lambda _: VMEM, outs),
        scratch_shapes=list(scratch),
        compiler_params=pltpu.CompilerParams(vmem_limit_bytes=16 << 20),
        cost_estimate=pl.CostEstimate(flops=flops, bytes_accessed=1 << 20, transcendentals=0),
    )(*ins)


def shape(dims, dtype):
    return jax.ShapeDtypeStruct(dims, dtype)


def shards(fields, interp, conv_weight, vert_weight, send_tiles, tile_pattern):
    members, level_len, columns = fields.shape
    tiles, tile_len, fine = interp.shape
    halo = vert_weight.shape[1] - 1
    rows = members * level_len
    patches = lax.axis_size("patch")
    levs = lax.axis_size("lev")
    tile_shape = (rows, tile_len)
    wide = tiles * tile_len
    tile_list = shape((tiles,) + tile_shape, F32)
    narrow_list = shape((tiles,) + tile_shape, BF16)
    edge_list = shape((members * halo, wide), BF16)
    block_list = shape((tiles, tile_len, wide), BF16)
    four = shape((4,) + tile_shape, BF16)

    def swap(block, start):
        partner = [
            (i, (i + 2) % patches if (i - start) % 4 < 2 else (i - 2) % patches)
            for i in range(patches)
        ]
        return lax.ppermute(block, "patch", partner)

    coarse, top, bottom, weights = call(
        functools.partial(restrict_kernel, halo),
        (
            shape((rows, wide), BF16),
            edge_list,
            edge_list,
            shape(vert_weight.shape[::-1], F32),
        ),
        [HBM] * 3,
        [in_hbm(array) for array in (fields, interp, vert_weight.T)],
        [
            pltpu.VMEM(fields.shape, BF16),
            pltpu.VMEM((tiles, tile_len, fine), BF16),
            pltpu.SemaphoreType.DMA((3,)),
        ],
    )
    low = lax.ppermute(top, "lev", [(i, i + 1) for i in range(levs - 1)])
    high = lax.ppermute(bottom, "lev", [(i + 1, i) for i in range(levs - 1)])
    partial, halo_matrix, own_blocks, received_blocks = call(
        functools.partial(vertical_kernel, level_len, halo),
        (
            shape((rows, wide), F32),
            shape((rows, 4 * members * halo), BF16),
            block_list,
            block_list,
        ),
        [VMEM] * 2 + [HBM] * 2,
        (coarse, weights, in_hbm(tile_pattern), in_hbm(conv_weight)),
        [
            pltpu.VMEM(conv_weight.shape, BF16),
            pltpu.SMEM(tile_pattern.shape, jnp.int32),
            pltpu.SemaphoreType.DMA((2,)),
        ],
    )
    sem = pltpu.SemaphoreType.DMA
    vertical, second, first = call(
        adjoint_kernel,
        (shape((rows, wide), BF16), four, four),
        [VMEM] * 5,
        (partial, halo_matrix, low, high, received_blocks),
    )
    from_second = swap(second, 2)
    from_first = swap(first, 0)
    own = call(own_kernel, tile_list, [VMEM] * 2, (vertical, own_blocks))
    links = pltpu.SMEM(send_tiles.shape, jnp.int32)
    payload = call(
        partner_kernel,
        shape((9,) + tile_shape, BF16),
        [VMEM] * 6,
        (send_tiles, own, second, first, from_second, from_first),
        [links, sem],
    )
    arrived = lax.ppermute(payload, "patch", [(i, i ^ 1) for i in range(patches)])
    total = call(
        gather_kernel,
        tile_list,
        [SMEM] + [VMEM] * 3,
        (send_tiles, own, from_second, from_first),
    )
    smooth, second, first = call(
        complete_kernel,
        (narrow_list, four, four),
        [VMEM] * 4,
        (send_tiles, total, payload, arrived),
        [pltpu.VMEM((tiles,) + tile_shape, F32), links, sem],
    )
    from_second = swap(second, 2)
    from_first = swap(first, 0)
    partial = call(
        own_forward_kernel, shape((rows, wide), F32), [VMEM] * 2, (smooth, own_blocks)
    )
    return call(
        forward_kernel,
        shape(fields.shape, F32),
        [VMEM] * 7,
        (partial, second, first, from_second, from_first, received_blocks, interp),
        [pltpu.VMEM((rows, wide), BF16), pltpu.VMEM((rows, wide), BF16)],
    )


def solution(mesh):
    in_specs = (
        P(None, "lev", "patch"),
        P("patch", None, None),
        P("patch", None, None, None),
        P(),
        P("patch", None, None),
        P("patch", None),
    )
    out_specs = P(None, "lev", "patch")
    return jax.shard_map(shards, mesh=mesh, in_specs=in_specs, out_specs=out_specs, check_vma=False)
```

```python
import functools

import jax
import jax.numpy as jnp
from jax import lax
from jax.experimental import pallas as pl
from jax.experimental.pallas import tpu as pltpu
from jax.sharding import PartitionSpec as P

BF16 = jnp.bfloat16
F32 = jnp.float32
HIGHEST = lax.Precision.HIGHEST


def nn(a, b):
    return lax.dot_general(a, b, (((1,), (0,)), ((), ())), preferred_element_type=F32)


def nt(a, b):
    return lax.dot_general(a, b, (((1,), (1,)), ((), ())), preferred_element_type=F32)


def lanes(t, width):
    return slice(t * width, (t + 1) * width)


def iota(shape, dim):
    return lax.broadcasted_iota(jnp.int32, shape, dim)


def split(a):
    high = a.astype(BF16)
    return high, (a - high.astype(F32)).astype(BF16)


def restrict_kernel(
    halo, fields, interp, weights, coarse, top, bottom, weights_copy,
    block, bases, sems
):
    tiles, tile_len, fine = bases.shape
    members, level_len, _ = block.shape
    rows = members * level_len
    pairs = ((interp, bases), (fields, block), (weights, weights_copy))
    copies = [
        pltpu.make_async_copy(source, target, sems.at[i])
        for i, (source, target) in enumerate(pairs)
    ]
    for copy in copies:
        copy.start()
    first_half = iota((members // 2, 2 * halo, tile_len), 1) < halo
    for copy in copies[:2]:
        copy.wait()
    for t in range(tiles):
        span = slice(t * fine, (t + 1) * fine)
        value = nt(block[:, :, span].reshape(rows, fine), bases[t])
        coarse[:, lanes(t, tile_len)] = value.astype(BF16)
        group = value.reshape(members // 2, 2, level_len, tile_len)
        even, odd = group[:, 0, : 2 * halo], group[:, 1, : 2 * halo]
        bottom[:, lanes(t, tile_len)] = (
            jnp.where(first_half, even, pltpu.roll(odd, halo, 1))
            .reshape(members * halo, tile_len)
            .astype(BF16)
        )
        even, odd = group[:, 0, level_len - 2 * halo :], group[:, 1, level_len - 2 * halo :]
        top[:, lanes(t, tile_len)] = (
            jnp.where(first_half, pltpu.roll(even, halo, 1), odd)
            .reshape(members * halo, tile_len)
            .astype(BF16)
        )
    for copy in copies[2:]:
        copy.wait()


def fetch_weights(pattern, conv, table, conv_copy, sems):
    fetches = (
        pltpu.make_async_copy(pattern, table, sems.at[0]),
        pltpu.make_async_copy(conv, conv_copy, sems.at[1]),
    )
    for fetch in fetches:
        fetch.start()
    return fetches


def lay_blocks(fetches, table, conv_copy, blocks, first_entry):
    tiles, count, tile_len, _ = conv_copy.shape
    spare = blocks.shape[0] - 1
    for fetch in fetches:
        fetch.wait()
    for t in range(tiles):
        for k in range(count):
            entry = table[t, k] - first_entry
            entry = jnp.where((entry >= 0) & (entry < spare), entry, spare)
            blocks[entry, :, lanes(t, tile_len)] = conv_copy[t, k]


def vertical_kernel(
    level_len, halo, coarse, weights, pattern, conv, partial, halo_matrix, received_blocks,
    conv_copy, table, sems
):
    fetches = fetch_weights(pattern, conv, table, conv_copy, sems)
    received_blocks[...] = jnp.zeros_like(received_blocks)
    rows = coarse.shape[0]
    halo_rows = rows // level_len * halo
    taps, levels = weights.shape
    half = taps // 2
    start = lax.axis_index("lev") * level_len
    distance = iota((levels, levels), 0) - iota((levels, levels), 1)
    taken = weights[...]
    band = jnp.zeros((levels, levels), F32)
    for j in range(taps):
        band = band + jnp.where(distance == j - half, taken[j : j + 1, :], 0.0)
    both = lax.dot_general(
        band, band, (((0,), (0,)), ((), ())), precision=HIGHEST, preferred_element_type=F32
    )
    pick = (
        iota((rows, levels), 1) == start + iota((rows, levels), 0) % level_len
    ).astype(BF16)
    place = iota((2 * halo_rows, levels), 0)
    level = jnp.where(
        place < halo_rows, start - halo + place % halo, start + level_len + place % halo
    )
    pick_halo = (iota((2 * halo_rows, levels), 1) == level).astype(BF16)
    same = iota((rows, rows), 0) // level_len == iota((rows, rows), 1) // level_len
    column = iota((rows, 2 * halo_rows), 1) % halo_rows
    same_halo = iota((rows, 2 * halo_rows), 0) // level_len == column // halo
    own_parts = []
    for i, part in enumerate(split(both)):
        chosen = nn(pick, part).astype(BF16)
        own_parts.append(jnp.where(same, nt(chosen, pick), 0.0).astype(BF16))
        halo_matrix[:, i * 2 * halo_rows : (i + 1) * 2 * halo_rows] = jnp.where(
            same_halo, nt(chosen, pick_halo), 0.0
        ).astype(BF16)
    own_matrix = jnp.concatenate(own_parts, axis=1)
    value = coarse[...]
    partial[...] = nn(own_matrix, jnp.concatenate([value, value], axis=0))
    lay_blocks(fetches, table, conv_copy, received_blocks, conv.shape[0])


def by_chip(body, first, second):
    odd = lax.axis_index("patch") // 2 % 2

    @pl.when(odd == 0)
    def _():
        body(second, first)

    @pl.when(odd == 1)
    def _():
        body(first, second)


def flat(blocks):
    entries = blocks.shape[0] - 1
    return blocks[:entries].reshape(-1, blocks.shape[-1])


def adjoint_kernel(partial, halo_matrix, low, high, received_blocks, smooth, second, first):
    tile_len = received_blocks.shape[1]
    edge = jnp.concatenate([low[...], high[...]], axis=0)
    value = (
        partial[...] + nn(halo_matrix[...], jnp.concatenate([edge, edge], axis=0))
    ).astype(BF16)
    smooth[...] = value
    returning = nt(value, flat(received_blocks)).astype(BF16)

    def sides(down, up):
        for i in range(4):
            up[i] = returning[:, lanes(i, tile_len)]
            down[i] = returning[:, lanes(4 + (i + 2) % 4, tile_len)]

    by_chip(sides, first, second)


def own_kernel(smooth, pattern, conv, own, blocks, conv_copy, table, sems):
    fetches = fetch_weights(pattern, conv, table, conv_copy, sems)
    blocks[...] = jnp.zeros_like(blocks)
    lay_blocks(fetches, table, conv_copy, blocks, 0)
    value = nt(smooth[...], flat(blocks))
    for t in range(own.shape[0]):
        own[t] = value[:, lanes(t, own.shape[2])]


def add_to(total, tile, piece):
    last = total.shape[0] - 1
    total[jnp.minimum(tile, last)] += jnp.where(tile <= last, piece.astype(F32), 0.0)


def partner_kernel(send, own, second, first, from_second, from_first, payload, table, sem):
    tiles = own.shape[0]
    core = lax.axis_index("patch") % 2
    fetch = pltpu.make_async_copy(send, table, sem)
    fetch.start()

    def copies(low, high):
        (down, from_low), (up, from_high) = low, high

        @pl.when(core == 0)
        def _():
            payload[0:2] = up[2:4]
            payload[2:4] = from_high[2:4]

        @pl.when(core == 1)
        def _():
            payload[0:2] = from_low[2:4]
            payload[2:4] = down[2:4]

    by_chip(copies, (first, from_first), (second, from_second))
    fetch.wait()
    for i in range(4):
        tile = table[0, 1 + i // 2, i % 2]
        payload[8, 16 * i : 16 * i + 16, :] = jnp.full(
            (16, payload.shape[2]), tile.astype(F32)
        ).astype(BF16)

    def sums(from_low, from_high):
        for i in range(4):
            tile = table[0, 1 + i // 2, i % 2]
            value = own[jnp.minimum(tile, tiles - 1)]
            for back in range(2):
                for link, source in ((0, from_low), (3, from_high)):
                    value = value + jnp.where(
                        table[0, link, back] == tile, source[back].astype(F32), 0.0
                    )
            payload[4 + i] = value.astype(BF16)

    by_chip(sums, from_first, from_second)


def gather_kernel(send, own, from_second, from_first, total):
    total[...] = own[...]

    def sides(from_low, from_high):
        for s in range(2):
            add_to(total, send[0, 0, s], from_low[s])
            add_to(total, send[0, 3, s], from_high[s])

    by_chip(sides, from_first, from_second)


def complete_kernel(
    send, partial, payload, arrived, smooth, second, first, total, table, sem
):
    tiles = partial.shape[0]
    fetch = pltpu.make_async_copy(send, table, sem)
    fetch.start()
    total[...] = partial[...]
    marks = [arrived[8, 16 * i : 16 * i + 1, :].astype(F32) for i in range(4)]
    pieces = [payload[i].astype(F32) for i in range(4)]
    theirs = []
    for i in range(4):
        tile = arrived[4 + i].astype(F32) + pieces[i]
        for j in (2, 3) if i < 2 else (0, 1):
            tile = tile + jnp.where(marks[i] == marks[j], pieces[j], 0.0)
        theirs.append(tile.astype(BF16))

    def forwarded(down, up):
        for s in range(2):
            down[2 + s] = theirs[s]
            up[2 + s] = theirs[2 + s]

    by_chip(forwarded, first, second)
    fetch.wait()
    for i in range(4):
        add_to(total, table[0, 1 + i // 2, i % 2], arrived[i])
    smooth[...] = total[...].astype(BF16)

    def sides(down, up):
        for s in range(2):
            down[s] = smooth[jnp.minimum(table[0, 0, s], tiles - 1)]
            up[s] = smooth[jnp.minimum(table[0, 3, s], tiles - 1)]

    by_chip(sides, first, second)


def own_forward_kernel(smooth, own_blocks, partial):
    tiles = smooth.shape[0]
    picked = jnp.concatenate([smooth[t] for t in range(tiles)], axis=1)
    partial[...] = nn(picked, flat(own_blocks))


def forward_kernel(
    partial, second, first, from_second, from_first, received_blocks, interp, out, entries, mixed
):
    tiles, tile_len, fine = interp.shape
    members, level_len, _ = out.shape
    core = lax.axis_index("patch") % 2

    def put(place, source):
        for i in range(2):
            entries[:, lanes(place + i, tile_len)] = source[i]

    def sides(low, high):
        (down, from_low), (up, from_high) = low, high
        put(0, from_high.at[0:2])
        put(6, from_low.at[0:2])

        @pl.when(core == 0)
        def _():
            put(2, down.at[2:4])
            put(4, from_low.at[2:4])

        @pl.when(core == 1)
        def _():
            put(2, from_high.at[2:4])
            put(4, up.at[2:4])

    by_chip(sides, (first, from_first), (second, from_second))
    mixed[...] = (partial[...] + nn(entries[...], flat(received_blocks))).astype(BF16)
    for t in range(tiles):
        out[:, :, lanes(t, fine)] = nn(mixed[:, lanes(t, tile_len)], interp[t]).reshape(
            members, level_len, fine
        )


VMEM = pl.BlockSpec(memory_space=pltpu.VMEM)
SMEM = pl.BlockSpec(memory_space=pltpu.SMEM)
HBM = pl.BlockSpec(memory_space=pltpu.HBM)


def in_hbm(array):
    return pltpu.with_memory_space_constraint(array, pltpu.HBM)


def call(kernel, outs, specs, ins, scratch=(), flops=1 << 24):
    return pl.pallas_call(
        kernel,
        out_shape=outs,
        in_specs=specs,
        out_specs=jax.tree.map(lambda _: VMEM, outs),
        scratch_shapes=list(scratch),
        compiler_params=pltpu.CompilerParams(vmem_limit_bytes=16 << 20),
        cost_estimate=pl.CostEstimate(flops=flops, bytes_accessed=1 << 20, transcendentals=0),
    )(*ins)


def shape(dims, dtype):
    return jax.ShapeDtypeStruct(dims, dtype)


def shards(fields, interp, conv_weight, vert_weight, send_tiles, tile_pattern):
    members, level_len, columns = fields.shape
    tiles, tile_len, fine = interp.shape
    halo = vert_weight.shape[1] - 1
    rows = members * level_len
    patches = lax.axis_size("patch")
    levs = lax.axis_size("lev")
    tile_shape = (rows, tile_len)
    wide = tiles * tile_len
    tile_list = shape((tiles,) + tile_shape, F32)
    narrow_list = shape((tiles,) + tile_shape, BF16)
    edge_list = shape((members * halo, wide), BF16)
    block_list = shape((tiles + 1, tile_len, wide), BF16)
    four = shape((4,) + tile_shape, BF16)

    def swap(block, start):
        partner = [
            (i, (i + 2) % patches if (i - start) % 4 < 2 else (i - 2) % patches)
            for i in range(patches)
        ]
        return lax.ppermute(block, "patch", partner)

    coarse, top, bottom, weights = call(
        functools.partial(restrict_kernel, halo),
        (
            shape((rows, wide), BF16),
            edge_list,
            edge_list,
            shape(vert_weight.shape[::-1], F32),
        ),
        [HBM] * 3,
        [in_hbm(array) for array in (fields, interp, vert_weight.T)],
        [
            pltpu.VMEM(fields.shape, BF16),
            pltpu.VMEM((tiles, tile_len, fine), BF16),
            pltpu.SemaphoreType.DMA((3,)),
        ],
    )
    low = lax.ppermute(top, "lev", [(i, i + 1) for i in range(levs - 1)])
    high = lax.ppermute(bottom, "lev", [(i + 1, i) for i in range(levs - 1)])
    weight_scratch = [
        pltpu.VMEM(conv_weight.shape, BF16),
        pltpu.SMEM(tile_pattern.shape, jnp.int32),
        pltpu.SemaphoreType.DMA((2,)),
    ]
    partial, halo_matrix, received_blocks = call(
        functools.partial(vertical_kernel, level_len, halo),
        (shape((rows, wide), F32), shape((rows, 4 * members * halo), BF16), block_list),
        [VMEM] * 2 + [HBM] * 2,
        (coarse, weights, in_hbm(tile_pattern), in_hbm(conv_weight)),
        weight_scratch,
    )
    sem = pltpu.SemaphoreType.DMA
    vertical, second, first = call(
        adjoint_kernel,
        (shape((rows, wide), BF16), four, four),
        [VMEM] * 5,
        (partial, halo_matrix, low, high, received_blocks),
    )
    from_second = swap(second, 2)
    from_first = swap(first, 0)
    own, own_blocks = call(
        own_kernel,
        (tile_list, block_list),
        [VMEM] + [HBM] * 2,
        (vertical, in_hbm(tile_pattern), in_hbm(conv_weight)),
        weight_scratch,
    )
    links = pltpu.SMEM(send_tiles.shape, jnp.int32)
    payload = call(
        partner_kernel,
        shape((9,) + tile_shape, BF16),
        [VMEM] * 6,
        (send_tiles, own, second, first, from_second, from_first),
        [links, sem],
    )
    arrived = lax.ppermute(payload, "patch", [(i, i ^ 1) for i in range(patches)])
    total = call(
        gather_kernel,
        tile_list,
        [SMEM] + [VMEM] * 3,
        (send_tiles, own, from_second, from_first),
    )
    smooth, second, first = call(
        complete_kernel,
        (narrow_list, four, four),
        [VMEM] * 4,
        (send_tiles, total, payload, arrived),
        [pltpu.VMEM((tiles,) + tile_shape, F32), links, sem],
    )
    from_second = swap(second, 2)
    from_first = swap(first, 0)
    partial = call(
        own_forward_kernel, shape((rows, wide), F32), [VMEM] * 2, (smooth, own_blocks)
    )
    return call(
        forward_kernel,
        shape(fields.shape, F32),
        [VMEM] * 7,
        (partial, second, first, from_second, from_first, received_blocks, interp),
        [pltpu.VMEM((rows, wide), BF16), pltpu.VMEM((rows, wide), BF16)],
    )


def solution(mesh):
    in_specs = (
        P(None, "lev", "patch"),
        P("patch", None, None),
        P("patch", None, None, None),
        P(),
        P("patch", None, None),
        P("patch", None),
    )
    out_specs = P(None, "lev", "patch")
    return jax.shard_map(shards, mesh=mesh, in_specs=in_specs, out_specs=out_specs, check_vma=False)
```

```python
import functools

import jax
import jax.numpy as jnp
from jax import lax
from jax.experimental import pallas as pl
from jax.experimental.pallas import tpu as pltpu
from jax.sharding import PartitionSpec as P

BF16 = jnp.bfloat16
F32 = jnp.float32
HIGHEST = lax.Precision.HIGHEST


def nn(a, b):
    return lax.dot_general(a, b, (((1,), (0,)), ((), ())), preferred_element_type=F32)


def nt(a, b):
    return lax.dot_general(a, b, (((1,), (1,)), ((), ())), preferred_element_type=F32)


def lanes(t, width):
    return slice(t * width, (t + 1) * width)


def iota(shape, dim):
    return lax.broadcasted_iota(jnp.int32, shape, dim)


def split(a):
    high = a.astype(BF16)
    return high, (a - high.astype(F32)).astype(BF16)


def restrict_kernel(
    halo, fields, interp, weights, coarse, top, bottom, weights_copy,
    block, bases, sems
):
    tiles, tile_len, fine = bases.shape
    members, level_len, _ = block.shape
    rows = members * level_len
    half = tiles // 2
    parts = [pl.ds(i * half, half) for i in range(2)]
    columns = [pl.ds(i * half * fine, half * fine) for i in range(2)]
    pairs = [(interp.at[parts[0]], bases.at[parts[0]])]
    pairs += [(fields.at[:, :, columns[0]], block.at[:, :, columns[0]])]
    pairs += [(interp.at[parts[1]], bases.at[parts[1]])]
    pairs += [(fields.at[:, :, columns[1]], block.at[:, :, columns[1]])]
    pairs += [(weights, weights_copy)]
    copies = [
        pltpu.make_async_copy(source, target, sems.at[i])
        for i, (source, target) in enumerate(pairs)
    ]
    for copy in copies:
        copy.start()
    first_half = iota((members // 2, 2 * halo, tile_len), 1) < halo
    for t in range(tiles):
        if t % half == 0:
            for copy in copies[2 * (t // half) : 2 * (t // half) + 2]:
                copy.wait()
        span = slice(t * fine, (t + 1) * fine)
        value = nt(block[:, :, span].reshape(rows, fine), bases[t])
        coarse[:, lanes(t, tile_len)] = value.astype(BF16)
        group = value.reshape(members // 2, 2, level_len, tile_len)
        even, odd = group[:, 0, : 2 * halo], group[:, 1, : 2 * halo]
        bottom[:, lanes(t, tile_len)] = (
            jnp.where(first_half, even, pltpu.roll(odd, halo, 1))
            .reshape(members * halo, tile_len)
            .astype(BF16)
        )
        even, odd = group[:, 0, level_len - 2 * halo :], group[:, 1, level_len - 2 * halo :]
        top[:, lanes(t, tile_len)] = (
            jnp.where(first_half, pltpu.roll(even, halo, 1), odd)
            .reshape(members * halo, tile_len)
            .astype(BF16)
        )
    copies[4].wait()


def fetch_weights(pattern, conv, table, conv_copy, sems):
    fetches = (
        pltpu.make_async_copy(pattern, table, sems.at[0]),
        pltpu.make_async_copy(conv, conv_copy, sems.at[1]),
    )
    for fetch in fetches:
        fetch.start()
    return fetches


def lay_blocks(fetches, table, conv_copy, blocks, first_entry):
    tiles, count, tile_len, _ = conv_copy.shape
    spare = blocks.shape[0] - 1
    for fetch in fetches:
        fetch.wait()
    for t in range(tiles):
        for k in range(count):
            entry = table[t, k] - first_entry

            @pl.when((entry >= 0) & (entry < spare))
            def _():
                blocks[entry, :, lanes(t, tile_len)] = conv_copy[t, k]


def vertical_kernel(
    level_len, halo, coarse, weights, pattern, conv, partial, halo_matrix, received_blocks,
    conv_copy, table, sems
):
    fetches = fetch_weights(pattern, conv, table, conv_copy, sems)
    received_blocks[...] = jnp.zeros_like(received_blocks)
    rows = coarse.shape[0]
    halo_rows = rows // level_len * halo
    taps, levels = weights.shape
    half = taps // 2
    start = lax.axis_index("lev") * level_len
    distance = iota((levels, levels), 0) - iota((levels, levels), 1)
    taken = weights[...]
    band = jnp.zeros((levels, levels), F32)
    for j in range(taps):
        band = band + jnp.where(distance == j - half, taken[j : j + 1, :], 0.0)
    both = lax.dot_general(
        band, band, (((0,), (0,)), ((), ())), precision=HIGHEST, preferred_element_type=F32
    )
    pick = (
        iota((rows, levels), 1) == start + iota((rows, levels), 0) % level_len
    ).astype(BF16)
    place = iota((2 * halo_rows, levels), 0)
    level = jnp.where(
        place < halo_rows, start - halo + place % halo, start + level_len + place % halo
    )
    pick_halo = (iota((2 * halo_rows, levels), 1) == level).astype(BF16)
    same = iota((rows, rows), 0) // level_len == iota((rows, rows), 1) // level_len
    column = iota((rows, 2 * halo_rows), 1) % halo_rows
    same_halo = iota((rows, 2 * halo_rows), 0) // level_len == column // halo
    own_parts = []
    for i, part in enumerate(split(both)):
        chosen = nn(pick, part).astype(BF16)
        own_parts.append(jnp.where(same, nt(chosen, pick), 0.0).astype(BF16))
        halo_matrix[:, i * 2 * halo_rows : (i + 1) * 2 * halo_rows] = jnp.where(
            same_halo, nt(chosen, pick_halo), 0.0
        ).astype(BF16)
    own_matrix = jnp.concatenate(own_parts, axis=1)
    value = coarse[...]
    partial[...] = nn(own_matrix, jnp.concatenate([value, value], axis=0))
    lay_blocks(fetches, table, conv_copy, received_blocks, conv.shape[0])


def by_chip(body, first, second):
    odd = lax.axis_index("patch") // 2 % 2

    @pl.when(odd == 0)
    def _():
        body(second, first)

    @pl.when(odd == 1)
    def _():
        body(first, second)


def flat(blocks):
    entries = blocks.shape[0] - 1
    return blocks[:entries].reshape(-1, blocks.shape[-1])


def adjoint_kernel(partial, halo_matrix, high, low, received_blocks, smooth, second, first):
    tile_len = received_blocks.shape[1]
    edge = jnp.concatenate([low[...], high[...]], axis=0)
    value = (
        partial[...] + nn(halo_matrix[...], jnp.concatenate([edge, edge], axis=0))
    ).astype(BF16)
    smooth[...] = value
    returning = nt(value, flat(received_blocks)).astype(BF16)

    def sides(down, up):
        for i in range(4):
            up[i] = returning[:, lanes(i, tile_len)]
            down[i] = returning[:, lanes(4 + (i + 2) % 4, tile_len)]

    by_chip(sides, first, second)


def own_kernel(smooth, pattern, conv, own, blocks, conv_copy, table, sems):
    fetches = fetch_weights(pattern, conv, table, conv_copy, sems)
    blocks[...] = jnp.zeros_like(blocks)
    lay_blocks(fetches, table, conv_copy, blocks, 0)
    value = nt(smooth[...], flat(blocks))
    for t in range(own.shape[0]):
        own[t] = value[:, lanes(t, own.shape[2])]


def add_to(total, tile, piece):
    last = total.shape[0] - 1
    total[jnp.minimum(tile, last)] += jnp.where(tile <= last, piece.astype(F32), 0.0)


def partner_kernel(send, own, second, first, from_second, from_first, payload, table, sem):
    tiles = own.shape[0]
    core = lax.axis_index("patch") % 2
    fetch = pltpu.make_async_copy(send, table, sem)
    fetch.start()

    def copies(low, high):
        (down, from_low), (up, from_high) = low, high

        @pl.when(core == 0)
        def _():
            payload[0:2] = up[2:4]
            payload[2:4] = from_high[2:4]

        @pl.when(core == 1)
        def _():
            payload[0:2] = from_low[2:4]
            payload[2:4] = down[2:4]

    by_chip(copies, (first, from_first), (second, from_second))
    fetch.wait()
    for i in range(4):
        tile = table[0, 1 + i // 2, i % 2]
        payload[8, 16 * i : 16 * i + 16, :] = jnp.full(
            (16, payload.shape[2]), tile.astype(F32)
        ).astype(BF16)

    def sums(from_low, from_high):
        for i in range(4):
            tile = table[0, 1 + i // 2, i % 2]
            value = own[jnp.minimum(tile, tiles - 1)]
            for back in range(2):
                for link, source in ((0, from_low), (3, from_high)):
                    value = value + jnp.where(
                        table[0, link, back] == tile, source[back].astype(F32), 0.0
                    )
            payload[4 + i] = value.astype(BF16)

    by_chip(sums, from_first, from_second)


def gather_kernel(send, own, from_second, from_first, total):
    total[...] = own[...]

    def sides(from_low, from_high):
        for s in range(2):
            add_to(total, send[0, 0, s], from_low[s])
            add_to(total, send[0, 3, s], from_high[s])

    by_chip(sides, from_first, from_second)


def complete_kernel(
    send, partial, payload, arrived, smooth, second, first, total, table, sem
):
    tiles = partial.shape[0]
    fetch = pltpu.make_async_copy(send, table, sem)
    fetch.start()
    total[...] = partial[...]
    marks = [arrived[8, 16 * i : 16 * i + 1, :].astype(F32) for i in range(4)]
    pieces = [payload[i].astype(F32) for i in range(4)]
    theirs = []
    for i in range(4):
        tile = arrived[4 + i].astype(F32) + pieces[i]
        for j in (2, 3) if i < 2 else (0, 1):
            tile = tile + jnp.where(marks[i] == marks[j], pieces[j], 0.0)
        theirs.append(tile.astype(BF16))

    def forwarded(down, up):
        for s in range(2):
            down[2 + s] = theirs[s]
            up[2 + s] = theirs[2 + s]

    by_chip(forwarded, first, second)
    fetch.wait()
    for i in range(4):
        add_to(total, table[0, 1 + i // 2, i % 2], arrived[i])
    smooth[...] = total[...].astype(BF16)

    def sides(down, up):
        for s in range(2):
            down[s] = smooth[jnp.minimum(table[0, 0, s], tiles - 1)]
            up[s] = smooth[jnp.minimum(table[0, 3, s], tiles - 1)]

    by_chip(sides, first, second)


def own_forward_kernel(smooth, own_blocks, partial):
    tiles = smooth.shape[0]
    picked = jnp.concatenate([smooth[t] for t in range(tiles)], axis=1)
    partial[...] = nn(picked, flat(own_blocks))


def forward_kernel(
    partial, second, first, from_second, from_first, received_blocks, interp, out, entries, mixed
):
    tiles, tile_len, fine = interp.shape
    members, level_len, _ = out.shape
    core = lax.axis_index("patch") % 2

    def put(place, source):
        for i in range(2):
            entries[:, lanes(place + i, tile_len)] = source[i]

    def sides(low, high):
        (down, from_low), (up, from_high) = low, high
        put(0, from_high.at[0:2])
        put(6, from_low.at[0:2])

        @pl.when(core == 0)
        def _():
            put(2, down.at[2:4])
            put(4, from_low.at[2:4])

        @pl.when(core == 1)
        def _():
            put(2, from_high.at[2:4])
            put(4, up.at[2:4])

    by_chip(sides, (first, from_first), (second, from_second))
    mixed[...] = (partial[...] + nn(entries[...], flat(received_blocks))).astype(BF16)
    for t in range(tiles):
        out[:, :, lanes(t, fine)] = nn(mixed[:, lanes(t, tile_len)], interp[t]).reshape(
            members, level_len, fine
        )


VMEM = pl.BlockSpec(memory_space=pltpu.VMEM)
SMEM = pl.BlockSpec(memory_space=pltpu.SMEM)
HBM = pl.BlockSpec(memory_space=pltpu.HBM)


def in_hbm(array):
    return pltpu.with_memory_space_constraint(array, pltpu.HBM)


def call(kernel, outs, specs, ins, scratch=(), flops=1 << 24):
    return pl.pallas_call(
        kernel,
        out_shape=outs,
        in_specs=specs,
        out_specs=jax.tree.map(lambda _: VMEM, outs),
        scratch_shapes=list(scratch),
        compiler_params=pltpu.CompilerParams(vmem_limit_bytes=16 << 20),
        cost_estimate=pl.CostEstimate(flops=flops, bytes_accessed=1 << 20, transcendentals=0),
    )(*ins)


def shape(dims, dtype):
    return jax.ShapeDtypeStruct(dims, dtype)


def shards(fields, interp, conv_weight, vert_weight, send_tiles, tile_pattern):
    members, level_len, columns = fields.shape
    tiles, tile_len, fine = interp.shape
    halo = vert_weight.shape[1] - 1
    rows = members * level_len
    patches = lax.axis_size("patch")
    levs = lax.axis_size("lev")
    tile_shape = (rows, tile_len)
    wide = tiles * tile_len
    tile_list = shape((tiles,) + tile_shape, F32)
    narrow_list = shape((tiles,) + tile_shape, BF16)
    edge_list = shape((members * halo, wide), BF16)
    block_list = shape((tiles + 1, tile_len, wide), BF16)
    four = shape((4,) + tile_shape, BF16)

    def swap(block, start):
        partner = [
            (i, (i + 2) % patches if (i - start) % 4 < 2 else (i - 2) % patches)
            for i in range(patches)
        ]
        return lax.ppermute(block, "patch", partner)

    coarse, top, bottom, weights = call(
        functools.partial(restrict_kernel, halo),
        (
            shape((rows, wide), BF16),
            edge_list,
            edge_list,
            shape(vert_weight.shape[::-1], F32),
        ),
        [HBM] * 3,
        [in_hbm(array) for array in (fields, interp, vert_weight.T)],
        [
            pltpu.VMEM(fields.shape, BF16),
            pltpu.VMEM((tiles, tile_len, fine), BF16),
            pltpu.SemaphoreType.DMA((5,)),
        ],
    )
    low = lax.ppermute(top, "lev", [(i, i + 1) for i in range(levs - 1)])
    high = lax.ppermute(bottom, "lev", [(i + 1, i) for i in range(levs - 1)])
    weight_scratch = [
        pltpu.VMEM(conv_weight.shape, BF16),
        pltpu.SMEM(tile_pattern.shape, jnp.int32),
        pltpu.SemaphoreType.DMA((2,)),
    ]
    partial, halo_matrix, received_blocks = call(
        functools.partial(vertical_kernel, level_len, halo),
        (shape((rows, wide), F32), shape((rows, 4 * members * halo), BF16), block_list),
        [VMEM] * 2 + [HBM] * 2,
        (coarse, weights, in_hbm(tile_pattern), in_hbm(conv_weight)),
        weight_scratch,
    )
    sem = pltpu.SemaphoreType.DMA
    vertical, second, first = call(
        adjoint_kernel,
        (shape((rows, wide), BF16), four, four),
        [VMEM] * 5,
        (partial, halo_matrix, high, low, received_blocks),
    )
    from_second = swap(second, 2)
    from_first = swap(first, 0)
    own, own_blocks = call(
        own_kernel,
        (tile_list, block_list),
        [VMEM] + [HBM] * 2,
        (vertical, in_hbm(tile_pattern), in_hbm(conv_weight)),
        weight_scratch,
    )
    links = pltpu.SMEM(send_tiles.shape, jnp.int32)
    payload = call(
        partner_kernel,
        shape((9,) + tile_shape, BF16),
        [VMEM] * 6,
        (send_tiles, own, second, first, from_second, from_first),
        [links, sem],
    )
    arrived = lax.ppermute(payload, "patch", [(i, i ^ 1) for i in range(patches)])
    total = call(
        gather_kernel,
        tile_list,
        [SMEM] + [VMEM] * 3,
        (send_tiles, own, from_second, from_first),
    )
    smooth, second, first = call(
        complete_kernel,
        (narrow_list, four, four),
        [VMEM] * 4,
        (send_tiles, total, payload, arrived),
        [pltpu.VMEM((tiles,) + tile_shape, F32), links, sem],
    )
    from_second = swap(second, 2)
    from_first = swap(first, 0)
    partial = call(
        own_forward_kernel, shape((rows, wide), F32), [VMEM] * 2, (smooth, own_blocks)
    )
    return call(
        forward_kernel,
        shape(fields.shape, F32),
        [VMEM] * 7,
        (partial, second, first, from_second, from_first, received_blocks, interp),
        [pltpu.VMEM((rows, wide), BF16), pltpu.VMEM((rows, wide), BF16)],
    )


def solution(mesh):
    in_specs = (
        P(None, "lev", "patch"),
        P("patch", None, None),
        P("patch", None, None, None),
        P(),
        P("patch", None, None),
        P("patch", None),
    )
    out_specs = P(None, "lev", "patch")
    return jax.shard_map(shards, mesh=mesh, in_specs=in_specs, out_specs=out_specs, check_vma=False)
```

```python
import functools

import jax
import jax.numpy as jnp
from jax import lax
from jax.experimental import pallas as pl
from jax.experimental.pallas import tpu as pltpu
from jax.sharding import PartitionSpec as P

BF16 = jnp.bfloat16
F32 = jnp.float32
HIGHEST = lax.Precision.HIGHEST


def nn(a, b):
    return lax.dot_general(a, b, (((1,), (0,)), ((), ())), preferred_element_type=F32)


def nt(a, b):
    return lax.dot_general(a, b, (((1,), (1,)), ((), ())), preferred_element_type=F32)


def lanes(t, width):
    return slice(t * width, (t + 1) * width)


def iota(shape, dim):
    return lax.broadcasted_iota(jnp.int32, shape, dim)


def split(a):
    high = a.astype(BF16)
    return high, (a - high.astype(F32)).astype(BF16)


def restrict_kernel(
    halo, fields, interp, weights, coarse, top, bottom, weights_copy,
    block, bases, sems
):
    tiles, tile_len, fine = bases.shape
    members, level_len, _ = block.shape
    rows = members * level_len
    half = tiles // 2
    parts = [pl.ds(i * half, half) for i in range(2)]
    columns = [pl.ds(i * half * fine, half * fine) for i in range(2)]
    pairs = [(interp.at[parts[0]], bases.at[parts[0]])]
    pairs += [(fields.at[:, :, columns[0]], block.at[:, :, columns[0]])]
    pairs += [(interp.at[parts[1]], bases.at[parts[1]])]
    pairs += [(fields.at[:, :, columns[1]], block.at[:, :, columns[1]])]
    pairs += [(weights, weights_copy)]
    copies = [
        pltpu.make_async_copy(source, target, sems.at[i])
        for i, (source, target) in enumerate(pairs)
    ]
    for copy in copies:
        copy.start()
    first_half = iota((members // 2, 2 * halo, tile_len), 1) < halo
    for t in range(tiles):
        if t % half == 0:
            for copy in copies[2 * (t // half) : 2 * (t // half) + 2]:
                copy.wait()
        span = slice(t * fine, (t + 1) * fine)
        value = nt(block[:, :, span].reshape(rows, fine), bases[t])
        coarse[:, lanes(t, tile_len)] = value.astype(BF16)
        group = value.reshape(members // 2, 2, level_len, tile_len)
        even, odd = group[:, 0, : 2 * halo], group[:, 1, : 2 * halo]
        bottom[:, lanes(t, tile_len)] = (
            jnp.where(first_half, even, pltpu.roll(odd, halo, 1))
            .reshape(members * halo, tile_len)
            .astype(BF16)
        )
        even, odd = group[:, 0, level_len - 2 * halo :], group[:, 1, level_len - 2 * halo :]
        top[:, lanes(t, tile_len)] = (
            jnp.where(first_half, pltpu.roll(even, halo, 1), odd)
            .reshape(members * halo, tile_len)
            .astype(BF16)
        )
    copies[4].wait()


def fetch_weights(pattern, conv, table, conv_copy, sems):
    fetches = (
        pltpu.make_async_copy(pattern, table, sems.at[0]),
        pltpu.make_async_copy(conv, conv_copy, sems.at[1]),
    )
    for fetch in fetches:
        fetch.start()
    return fetches


def lay_blocks(fetches, table, conv_copy, blocks, first_entry):
    tiles, count, tile_len, _ = conv_copy.shape
    spare = blocks.shape[0] - 1
    for fetch in fetches:
        fetch.wait()
    for t in range(tiles):
        for k in range(count):
            entry = table[t, k] - first_entry

            @pl.when((entry >= 0) & (entry < spare))
            def _():
                blocks[entry, :, lanes(t, tile_len)] = conv_copy[t, k]


def vertical_kernel(
    level_len, halo, coarse, weights, pattern, conv, partial, halo_matrix, received_blocks,
    conv_copy, table, sems
):
    fetches = fetch_weights(pattern, conv, table, conv_copy, sems)
    rows = coarse.shape[0]
    halo_rows = rows // level_len * halo
    taps, levels = weights.shape
    half = taps // 2
    start = lax.axis_index("lev") * level_len
    distance = iota((levels, levels), 0) - iota((levels, levels), 1)
    taken = weights[...]
    band = jnp.zeros((levels, levels), F32)
    for j in range(taps):
        band = band + jnp.where(distance == j - half, taken[j : j + 1, :], 0.0)
    both = lax.dot_general(
        band, band, (((0,), (0,)), ((), ())), precision=HIGHEST, preferred_element_type=F32
    )
    pick = (
        iota((rows, levels), 1) == start + iota((rows, levels), 0) % level_len
    ).astype(BF16)
    place = iota((2 * halo_rows, levels), 0)
    level = jnp.where(
        place < halo_rows, start - halo + place % halo, start + level_len + place % halo
    )
    pick_halo = (iota((2 * halo_rows, levels), 1) == level).astype(BF16)
    same = iota((rows, rows), 0) // level_len == iota((rows, rows), 1) // level_len
    column = iota((rows, 2 * halo_rows), 1) % halo_rows
    same_halo = iota((rows, 2 * halo_rows), 0) // level_len == column // halo
    own_parts = []
    for i, part in enumerate(split(both)):
        chosen = nn(pick, part).astype(BF16)
        own_parts.append(jnp.where(same, nt(chosen, pick), 0.0).astype(BF16))
        halo_matrix[:, i * 2 * halo_rows : (i + 1) * 2 * halo_rows] = jnp.where(
            same_halo, nt(chosen, pick_halo), 0.0
        ).astype(BF16)
    own_matrix = jnp.concatenate(own_parts, axis=1)
    value = coarse[...]
    partial[...] = nn(own_matrix, jnp.concatenate([value, value], axis=0))
    received_blocks[...] = jnp.zeros_like(received_blocks)
    lay_blocks(fetches, table, conv_copy, received_blocks, conv.shape[0])


def by_chip(body, first, second):
    odd = lax.axis_index("patch") // 2 % 2

    @pl.when(odd == 0)
    def _():
        body(second, first)

    @pl.when(odd == 1)
    def _():
        body(first, second)


def flat(blocks):
    entries = blocks.shape[0] - 1
    return blocks[:entries].reshape(-1, blocks.shape[-1])


def adjoint_kernel(partial, halo_matrix, high, low, received_blocks, smooth, second, first):
    tile_len = received_blocks.shape[1]
    edge = jnp.concatenate([low[...], high[...]], axis=0)
    value = (
        partial[...] + nn(halo_matrix[...], jnp.concatenate([edge, edge], axis=0))
    ).astype(BF16)
    smooth[...] = value
    returning = nt(value, flat(received_blocks)).astype(BF16)

    def sides(down, up):
        for i in range(4):
            up[i] = returning[:, lanes(i, tile_len)]
            down[i] = returning[:, lanes(4 + (i + 2) % 4, tile_len)]

    by_chip(sides, first, second)


def own_kernel(smooth, pattern, conv, own, blocks, conv_copy, table, sems):
    fetches = fetch_weights(pattern, conv, table, conv_copy, sems)
    blocks[...] = jnp.zeros_like(blocks)
    lay_blocks(fetches, table, conv_copy, blocks, 0)
    value = nt(smooth[...], flat(blocks))
    for t in range(own.shape[0]):
        own[t] = value[:, lanes(t, own.shape[2])]


def add_to(total, tile, piece):
    last = total.shape[0] - 1
    total[jnp.minimum(tile, last)] += jnp.where(tile <= last, piece.astype(F32), 0.0)


def partner_kernel(send, own, second, first, from_second, from_first, payload, table, sem):
    tiles = own.shape[0]
    core = lax.axis_index("patch") % 2
    fetch = pltpu.make_async_copy(send, table, sem)
    fetch.start()

    def copies(low, high):
        (down, from_low), (up, from_high) = low, high

        @pl.when(core == 0)
        def _():
            payload[0:2] = up[2:4]
            payload[2:4] = from_high[2:4]

        @pl.when(core == 1)
        def _():
            payload[0:2] = from_low[2:4]
            payload[2:4] = down[2:4]

    by_chip(copies, (first, from_first), (second, from_second))
    fetch.wait()
    for i in range(4):
        tile = table[0, 1 + i // 2, i % 2]
        payload[8, 16 * i : 16 * i + 16, :] = jnp.full(
            (16, payload.shape[2]), tile.astype(F32)
        ).astype(BF16)

    def sums(from_low, from_high):
        for i in range(4):
            tile = table[0, 1 + i // 2, i % 2]
            value = own[jnp.minimum(tile, tiles - 1)]
            for back in range(2):
                for link, source in ((0, from_low), (3, from_high)):
                    value = value + jnp.where(
                        table[0, link, back] == tile, source[back].astype(F32), 0.0
                    )
            payload[4 + i] = value.astype(BF16)

    by_chip(sums, from_first, from_second)


def gather_kernel(send, own, from_second, from_first, total):
    total[...] = own[...]

    def sides(from_low, from_high):
        for s in range(2):
            add_to(total, send[0, 0, s], from_low[s])
            add_to(total, send[0, 3, s], from_high[s])

    by_chip(sides, from_first, from_second)


def complete_kernel(
    send, partial, payload, arrived, smooth, second, first, total, table, sem
):
    tiles = partial.shape[0]
    fetch = pltpu.make_async_copy(send, table, sem)
    fetch.start()
    total[...] = partial[...]
    marks = [arrived[8, 16 * i : 16 * i + 1, :].astype(F32) for i in range(4)]
    pieces = [payload[i].astype(F32) for i in range(4)]
    theirs = []
    for i in range(4):
        tile = arrived[4 + i].astype(F32) + pieces[i]
        for j in (2, 3) if i < 2 else (0, 1):
            tile = tile + jnp.where(marks[i] == marks[j], pieces[j], 0.0)
        theirs.append(tile.astype(BF16))

    def forwarded(down, up):
        for s in range(2):
            down[2 + s] = theirs[s]
            up[2 + s] = theirs[2 + s]

    by_chip(forwarded, first, second)
    fetch.wait()
    for i in range(4):
        add_to(total, table[0, 1 + i // 2, i % 2], arrived[i])
    smooth[...] = total[...].astype(BF16)

    def sides(down, up):
        for s in range(2):
            down[s] = smooth[jnp.minimum(table[0, 0, s], tiles - 1)]
            up[s] = smooth[jnp.minimum(table[0, 3, s], tiles - 1)]

    by_chip(sides, first, second)


def own_forward_kernel(smooth, own_blocks, partial):
    tiles = smooth.shape[0]
    picked = jnp.concatenate([smooth[t] for t in range(tiles)], axis=1)
    partial[...] = nn(picked, flat(own_blocks))


def forward_kernel(
    partial, second, first, from_second, from_first, received_blocks, interp, out, entries, mixed
):
    tiles, tile_len, fine = interp.shape
    members, level_len, _ = out.shape
    core = lax.axis_index("patch") % 2

    def put(place, source):
        for i in range(2):
            entries[:, lanes(place + i, tile_len)] = source[i]

    def sides(low, high):
        (down, from_low), (up, from_high) = low, high
        put(0, from_high.at[0:2])
        put(6, from_low.at[0:2])

        @pl.when(core == 0)
        def _():
            put(2, down.at[2:4])
            put(4, from_low.at[2:4])

        @pl.when(core == 1)
        def _():
            put(2, from_high.at[2:4])
            put(4, up.at[2:4])

    by_chip(sides, (first, from_first), (second, from_second))
    mixed[...] = (partial[...] + nn(entries[...], flat(received_blocks))).astype(BF16)
    for t in range(tiles):
        out[:, :, lanes(t, fine)] = nn(mixed[:, lanes(t, tile_len)], interp[t]).reshape(
            members, level_len, fine
        )


VMEM = pl.BlockSpec(memory_space=pltpu.VMEM)
SMEM = pl.BlockSpec(memory_space=pltpu.SMEM)
HBM = pl.BlockSpec(memory_space=pltpu.HBM)


def in_hbm(array):
    return pltpu.with_memory_space_constraint(array, pltpu.HBM)


def call(kernel, outs, specs, ins, scratch=(), flops=1 << 24):
    return pl.pallas_call(
        kernel,
        out_shape=outs,
        in_specs=specs,
        out_specs=jax.tree.map(lambda _: VMEM, outs),
        scratch_shapes=list(scratch),
        compiler_params=pltpu.CompilerParams(vmem_limit_bytes=16 << 20),
        cost_estimate=pl.CostEstimate(flops=flops, bytes_accessed=1 << 20, transcendentals=0),
    )(*ins)


def shape(dims, dtype):
    return jax.ShapeDtypeStruct(dims, dtype)


def shards(fields, interp, conv_weight, vert_weight, send_tiles, tile_pattern):
    members, level_len, columns = fields.shape
    tiles, tile_len, fine = interp.shape
    halo = vert_weight.shape[1] - 1
    rows = members * level_len
    patches = lax.axis_size("patch")
    levs = lax.axis_size("lev")
    tile_shape = (rows, tile_len)
    wide = tiles * tile_len
    tile_list = shape((tiles,) + tile_shape, F32)
    narrow_list = shape((tiles,) + tile_shape, BF16)
    edge_list = shape((members * halo, wide), BF16)
    block_list = shape((tiles + 1, tile_len, wide), BF16)
    four = shape((4,) + tile_shape, BF16)

    def swap(block, start):
        partner = [
            (i, (i + 2) % patches if (i - start) % 4 < 2 else (i - 2) % patches)
            for i in range(patches)
        ]
        return lax.ppermute(block, "patch", partner)

    coarse, top, bottom, weights = call(
        functools.partial(restrict_kernel, halo),
        (
            shape((rows, wide), BF16),
            edge_list,
            edge_list,
            shape(vert_weight.shape[::-1], F32),
        ),
        [HBM] * 3,
        [in_hbm(array) for array in (fields, interp, vert_weight.T)],
        [
            pltpu.VMEM(fields.shape, BF16),
            pltpu.VMEM((tiles, tile_len, fine), BF16),
            pltpu.SemaphoreType.DMA((5,)),
        ],
    )
    low = lax.ppermute(top, "lev", [(i, i + 1) for i in range(levs - 1)])
    high = lax.ppermute(bottom, "lev", [(i + 1, i) for i in range(levs - 1)])
    weight_scratch = [
        pltpu.VMEM(conv_weight.shape, BF16),
        pltpu.SMEM(tile_pattern.shape, jnp.int32),
        pltpu.SemaphoreType.DMA((2,)),
    ]
    partial, halo_matrix, received_blocks = call(
        functools.partial(vertical_kernel, level_len, halo),
        (shape((rows, wide), F32), shape((rows, 4 * members * halo), BF16), block_list),
        [VMEM] * 2 + [HBM] * 2,
        (coarse, weights, in_hbm(tile_pattern), in_hbm(conv_weight)),
        weight_scratch,
    )
    sem = pltpu.SemaphoreType.DMA
    vertical, second, first = call(
        adjoint_kernel,
        (shape((rows, wide), BF16), four, four),
        [VMEM] * 5,
        (partial, halo_matrix, high, low, received_blocks),
    )
    from_second = swap(second, 2)
    from_first = swap(first, 0)
    own, own_blocks = call(
        own_kernel,
        (tile_list, block_list),
        [VMEM] + [HBM] * 2,
        (vertical, in_hbm(tile_pattern), in_hbm(conv_weight)),
        weight_scratch,
    )
    links = pltpu.SMEM(send_tiles.shape, jnp.int32)
    payload = call(
        partner_kernel,
        shape((9,) + tile_shape, BF16),
        [VMEM] * 6,
        (send_tiles, own, second, first, from_second, from_first),
        [links, sem],
    )
    arrived = lax.ppermute(payload, "patch", [(i, i ^ 1) for i in range(patches)])
    total = call(
        gather_kernel,
        tile_list,
        [SMEM] + [VMEM] * 3,
        (send_tiles, own, from_second, from_first),
    )
    smooth, second, first = call(
        complete_kernel,
        (narrow_list, four, four),
        [VMEM] * 4,
        (send_tiles, total, payload, arrived),
        [pltpu.VMEM((tiles,) + tile_shape, F32), links, sem],
    )
    from_second = swap(second, 2)
    from_first = swap(first, 0)
    partial = call(
        own_forward_kernel, shape((rows, wide), F32), [VMEM] * 2, (smooth, own_blocks)
    )
    return call(
        forward_kernel,
        shape(fields.shape, F32),
        [VMEM] * 7,
        (partial, second, first, from_second, from_first, received_blocks, interp),
        [pltpu.VMEM((rows, wide), BF16), pltpu.VMEM((rows, wide), BF16)],
    )


def solution(mesh):
    in_specs = (
        P(None, "lev", "patch"),
        P("patch", None, None),
        P("patch", None, None, None),
        P(),
        P("patch", None, None),
        P("patch", None),
    )
    out_specs = P(None, "lev", "patch")
    return jax.shard_map(shards, mesh=mesh, in_specs=in_specs, out_specs=out_specs, check_vma=False)
```

```python
import functools

import jax
import jax.numpy as jnp
from jax import lax
from jax.experimental import pallas as pl
from jax.experimental.pallas import tpu as pltpu
from jax.sharding import PartitionSpec as P

BF16 = jnp.bfloat16
F32 = jnp.float32
HIGHEST = lax.Precision.HIGHEST


def nn(a, b):
    return lax.dot_general(a, b, (((1,), (0,)), ((), ())), preferred_element_type=F32)


def nt(a, b):
    return lax.dot_general(a, b, (((1,), (1,)), ((), ())), preferred_element_type=F32)


def lanes(t, width):
    return slice(t * width, (t + 1) * width)


def iota(shape, dim):
    return lax.broadcasted_iota(jnp.int32, shape, dim)


def split(a):
    high = a.astype(BF16)
    return high, (a - high.astype(F32)).astype(BF16)


def restrict_kernel(
    halo, fields, interp, weights, coarse, top, bottom, weights_copy,
    block, bases, sems
):
    tiles, tile_len, fine = bases.shape
    members, level_len, _ = block.shape
    rows = members * level_len
    half = tiles // 2
    parts = [pl.ds(i * half, half) for i in range(2)]
    columns = [pl.ds(i * half * fine, half * fine) for i in range(2)]
    pairs = [(interp.at[parts[0]], bases.at[parts[0]])]
    pairs += [(fields.at[:, :, columns[0]], block.at[:, :, columns[0]])]
    pairs += [(interp.at[parts[1]], bases.at[parts[1]])]
    pairs += [(fields.at[:, :, columns[1]], block.at[:, :, columns[1]])]
    pairs += [(weights, weights_copy)]
    copies = [
        pltpu.make_async_copy(source, target, sems.at[i])
        for i, (source, target) in enumerate(pairs)
    ]
    for copy in copies:
        copy.start()
    first_half = iota((members // 2, 2 * halo, tile_len), 1) < halo
    for t in range(tiles):
        if t % half == 0:
            for copy in copies[2 * (t // half) : 2 * (t // half) + 2]:
                copy.wait()
        span = slice(t * fine, (t + 1) * fine)
        value = nt(block[:, :, span].reshape(rows, fine), bases[t])
        coarse[:, lanes(t, tile_len)] = value.astype(BF16)
        group = value.reshape(members // 2, 2, level_len, tile_len)
        even, odd = group[:, 0, : 2 * halo], group[:, 1, : 2 * halo]
        bottom[:, lanes(t, tile_len)] = (
            jnp.where(first_half, even, pltpu.roll(odd, halo, 1))
            .reshape(members * halo, tile_len)
            .astype(BF16)
        )
        even, odd = group[:, 0, level_len - 2 * halo :], group[:, 1, level_len - 2 * halo :]
        top[:, lanes(t, tile_len)] = (
            jnp.where(first_half, pltpu.roll(even, halo, 1), odd)
            .reshape(members * halo, tile_len)
            .astype(BF16)
        )
    copies[4].wait()


def fetch_weights(pattern, conv, table, conv_copy, sems):
    fetches = [pltpu.make_async_copy(pattern, table, sems.at[0])] + [
        pltpu.make_async_copy(conv.at[t], conv_copy.at[t], sems.at[1 + t])
        for t in range(conv.shape[0])
    ]
    for fetch in fetches:
        fetch.start()
    return fetches


def lay_blocks(fetches, table, conv_copy, blocks, first_entry):
    tiles, count, tile_len, _ = conv_copy.shape
    spare = blocks.shape[0] - 1
    fetches[0].wait()
    for t in range(tiles):
        fetches[1 + t].wait()
        for k in range(count):
            entry = table[t, k] - first_entry

            @pl.when((entry >= 0) & (entry < spare))
            def _():
                blocks[entry, :, lanes(t, tile_len)] = conv_copy[t, k]


def vertical_kernel(
    level_len, halo, coarse, weights, pattern, conv, partial, halo_matrix, received_blocks,
    conv_copy, table, sems
):
    fetches = fetch_weights(pattern, conv, table, conv_copy, sems)
    rows = coarse.shape[0]
    halo_rows = rows // level_len * halo
    taps, levels = weights.shape
    half = taps // 2
    start = lax.axis_index("lev") * level_len
    distance = iota((levels, levels), 0) - iota((levels, levels), 1)
    taken = weights[...]
    band = jnp.zeros((levels, levels), F32)
    for j in range(taps):
        band = band + jnp.where(distance == j - half, taken[j : j + 1, :], 0.0)
    both = lax.dot_general(
        band, band, (((0,), (0,)), ((), ())), precision=HIGHEST, preferred_element_type=F32
    )
    pick = (
        iota((rows, levels), 1) == start + iota((rows, levels), 0) % level_len
    ).astype(BF16)
    place = iota((2 * halo_rows, levels), 0)
    level = jnp.where(
        place < halo_rows, start - halo + place % halo, start + level_len + place % halo
    )
    pick_halo = (iota((2 * halo_rows, levels), 1) == level).astype(BF16)
    same = iota((rows, rows), 0) // level_len == iota((rows, rows), 1) // level_len
    column = iota((rows, 2 * halo_rows), 1) % halo_rows
    same_halo = iota((rows, 2 * halo_rows), 0) // level_len == column // halo
    own_parts = []
    for i, part in enumerate(split(both)):
        chosen = nn(pick, part).astype(BF16)
        own_parts.append(jnp.where(same, nt(chosen, pick), 0.0).astype(BF16))
        halo_matrix[:, i * 2 * halo_rows : (i + 1) * 2 * halo_rows] = jnp.where(
            same_halo, nt(chosen, pick_halo), 0.0
        ).astype(BF16)
    own_matrix = jnp.concatenate(own_parts, axis=1)
    value = coarse[...]
    partial[...] = nn(own_matrix, jnp.concatenate([value, value], axis=0))
    received_blocks[...] = jnp.zeros_like(received_blocks)
    lay_blocks(fetches, table, conv_copy, received_blocks, conv.shape[0])


def by_chip(body, first, second):
    odd = lax.axis_index("patch") // 2 % 2

    @pl.when(odd == 0)
    def _():
        body(second, first)

    @pl.when(odd == 1)
    def _():
        body(first, second)


def flat(blocks):
    entries = blocks.shape[0] - 1
    return blocks[:entries].reshape(-1, blocks.shape[-1])


def adjoint_kernel(partial, halo_matrix, high, low, received_blocks, smooth, second, first):
    tile_len = received_blocks.shape[1]
    edge = jnp.concatenate([low[...], high[...]], axis=0)
    value = (
        partial[...] + nn(halo_matrix[...], jnp.concatenate([edge, edge], axis=0))
    ).astype(BF16)
    smooth[...] = value
    returning = nt(value, flat(received_blocks)).astype(BF16)

    def sides(down, up):
        for i in range(4):
            up[i] = returning[:, lanes(i, tile_len)]
            down[i] = returning[:, lanes(4 + (i + 2) % 4, tile_len)]

    by_chip(sides, first, second)


def own_kernel(smooth, pattern, conv, own, blocks, conv_copy, table, sems):
    fetches = fetch_weights(pattern, conv, table, conv_copy, sems)
    blocks[...] = jnp.zeros_like(blocks)
    lay_blocks(fetches, table, conv_copy, blocks, 0)
    value = nt(smooth[...], flat(blocks))
    for t in range(own.shape[0]):
        own[t] = value[:, lanes(t, own.shape[2])]


def add_to(total, tile, piece):
    last = total.shape[0] - 1
    total[jnp.minimum(tile, last)] += jnp.where(tile <= last, piece.astype(F32), 0.0)


def partner_kernel(send, own, second, first, from_second, from_first, payload, table, sem):
    tiles = own.shape[0]
    core = lax.axis_index("patch") % 2
    fetch = pltpu.make_async_copy(send, table, sem)
    fetch.start()

    def copies(low, high):
        (down, from_low), (up, from_high) = low, high

        @pl.when(core == 0)
        def _():
            payload[0:2] = up[2:4]
            payload[2:4] = from_high[2:4]

        @pl.when(core == 1)
        def _():
            payload[0:2] = from_low[2:4]
            payload[2:4] = down[2:4]

    by_chip(copies, (first, from_first), (second, from_second))
    fetch.wait()
    for i in range(4):
        tile = table[0, 1 + i // 2, i % 2]
        payload[8, 16 * i : 16 * i + 16, :] = jnp.full(
            (16, payload.shape[2]), tile.astype(F32)
        ).astype(BF16)

    def sums(from_low, from_high):
        for i in range(4):
            tile = table[0, 1 + i // 2, i % 2]
            value = own[jnp.minimum(tile, tiles - 1)]
            for back in range(2):
                for link, source in ((0, from_low), (3, from_high)):
                    value = value + jnp.where(
                        table[0, link, back] == tile, source[back].astype(F32), 0.0
                    )
            payload[4 + i] = value.astype(BF16)

    by_chip(sums, from_first, from_second)


def gather_kernel(send, own, from_second, from_first, total):
    total[...] = own[...]

    def sides(from_low, from_high):
        for s in range(2):
            add_to(total, send[0, 0, s], from_low[s])
            add_to(total, send[0, 3, s], from_high[s])

    by_chip(sides, from_first, from_second)


def complete_kernel(
    send, partial, payload, arrived, smooth, second, first, total, table, sem
):
    tiles = partial.shape[0]
    fetch = pltpu.make_async_copy(send, table, sem)
    fetch.start()
    total[...] = partial[...]
    marks = [arrived[8, 16 * i : 16 * i + 1, :].astype(F32) for i in range(4)]
    pieces = [payload[i].astype(F32) for i in range(4)]
    theirs = []
    for i in range(4):
        tile = arrived[4 + i].astype(F32) + pieces[i]
        for j in (2, 3) if i < 2 else (0, 1):
            tile = tile + jnp.where(marks[i] == marks[j], pieces[j], 0.0)
        theirs.append(tile.astype(BF16))

    def forwarded(down, up):
        for s in range(2):
            down[2 + s] = theirs[s]
            up[2 + s] = theirs[2 + s]

    by_chip(forwarded, first, second)
    fetch.wait()
    for i in range(4):
        add_to(total, table[0, 1 + i // 2, i % 2], arrived[i])
    smooth[...] = total[...].astype(BF16)

    def sides(down, up):
        for s in range(2):
            down[s] = smooth[jnp.minimum(table[0, 0, s], tiles - 1)]
            up[s] = smooth[jnp.minimum(table[0, 3, s], tiles - 1)]

    by_chip(sides, first, second)


def own_forward_kernel(smooth, own_blocks, partial):
    tiles = smooth.shape[0]
    picked = jnp.concatenate([smooth[t] for t in range(tiles)], axis=1)
    partial[...] = nn(picked, flat(own_blocks))


def forward_kernel(
    partial, second, first, from_second, from_first, received_blocks, interp, out, entries, mixed
):
    tiles, tile_len, fine = interp.shape
    members, level_len, _ = out.shape
    core = lax.axis_index("patch") % 2

    def put(place, source):
        for i in range(2):
            entries[:, lanes(place + i, tile_len)] = source[i]

    def sides(low, high):
        (down, from_low), (up, from_high) = low, high
        put(0, from_high.at[0:2])
        put(6, from_low.at[0:2])

        @pl.when(core == 0)
        def _():
            put(2, down.at[2:4])
            put(4, from_low.at[2:4])

        @pl.when(core == 1)
        def _():
            put(2, from_high.at[2:4])
            put(4, up.at[2:4])

    by_chip(sides, (first, from_first), (second, from_second))
    mixed[...] = (partial[...] + nn(entries[...], flat(received_blocks))).astype(BF16)
    for t in range(tiles):
        out[:, :, lanes(t, fine)] = nn(mixed[:, lanes(t, tile_len)], interp[t]).reshape(
            members, level_len, fine
        )


VMEM = pl.BlockSpec(memory_space=pltpu.VMEM)
SMEM = pl.BlockSpec(memory_space=pltpu.SMEM)
HBM = pl.BlockSpec(memory_space=pltpu.HBM)


def in_hbm(array):
    return pltpu.with_memory_space_constraint(array, pltpu.HBM)


def call(kernel, outs, specs, ins, scratch=(), flops=1 << 24):
    return pl.pallas_call(
        kernel,
        out_shape=outs,
        in_specs=specs,
        out_specs=jax.tree.map(lambda _: VMEM, outs),
        scratch_shapes=list(scratch),
        compiler_params=pltpu.CompilerParams(vmem_limit_bytes=16 << 20),
        cost_estimate=pl.CostEstimate(flops=flops, bytes_accessed=1 << 20, transcendentals=0),
    )(*ins)


def shape(dims, dtype):
    return jax.ShapeDtypeStruct(dims, dtype)


def shards(fields, interp, conv_weight, vert_weight, send_tiles, tile_pattern):
    members, level_len, columns = fields.shape
    tiles, tile_len, fine = interp.shape
    halo = vert_weight.shape[1] - 1
    rows = members * level_len
    patches = lax.axis_size("patch")
    levs = lax.axis_size("lev")
    tile_shape = (rows, tile_len)
    wide = tiles * tile_len
    tile_list = shape((tiles,) + tile_shape, F32)
    narrow_list = shape((tiles,) + tile_shape, BF16)
    edge_list = shape((members * halo, wide), BF16)
    block_list = shape((tiles + 1, tile_len, wide), BF16)
    four = shape((4,) + tile_shape, BF16)

    def swap(block, start):
        partner = [
            (i, (i + 2) % patches if (i - start) % 4 < 2 else (i - 2) % patches)
            for i in range(patches)
        ]
        return lax.ppermute(block, "patch", partner)

    coarse, top, bottom, weights = call(
        functools.partial(restrict_kernel, halo),
        (
            shape((rows, wide), BF16),
            edge_list,
            edge_list,
            shape(vert_weight.shape[::-1], F32),
        ),
        [HBM] * 3,
        [in_hbm(array) for array in (fields, interp, vert_weight.T)],
        [
            pltpu.VMEM(fields.shape, BF16),
            pltpu.VMEM((tiles, tile_len, fine), BF16),
            pltpu.SemaphoreType.DMA((5,)),
        ],
    )
    low = lax.ppermute(top, "lev", [(i, i + 1) for i in range(levs - 1)])
    high = lax.ppermute(bottom, "lev", [(i + 1, i) for i in range(levs - 1)])
    weight_scratch = [
        pltpu.VMEM(conv_weight.shape, BF16),
        pltpu.SMEM(tile_pattern.shape, jnp.int32),
        pltpu.SemaphoreType.DMA((1 + tiles,)),
    ]
    partial, halo_matrix, received_blocks = call(
        functools.partial(vertical_kernel, level_len, halo),
        (shape((rows, wide), F32), shape((rows, 4 * members * halo), BF16), block_list),
        [VMEM] * 2 + [HBM] * 2,
        (coarse, weights, in_hbm(tile_pattern), in_hbm(conv_weight)),
        weight_scratch,
    )
    sem = pltpu.SemaphoreType.DMA
    vertical, second, first = call(
        adjoint_kernel,
        (shape((rows, wide), BF16), four, four),
        [VMEM] * 5,
        (partial, halo_matrix, high, low, received_blocks),
    )
    from_second = swap(second, 2)
    from_first = swap(first, 0)
    own, own_blocks = call(
        own_kernel,
        (tile_list, block_list),
        [VMEM] + [HBM] * 2,
        (vertical, in_hbm(tile_pattern), in_hbm(conv_weight)),
        weight_scratch,
    )
    links = pltpu.SMEM(send_tiles.shape, jnp.int32)
    payload = call(
        partner_kernel,
        shape((9,) + tile_shape, BF16),
        [VMEM] * 6,
        (send_tiles, own, second, first, from_second, from_first),
        [links, sem],
    )
    arrived = lax.ppermute(payload, "patch", [(i, i ^ 1) for i in range(patches)])
    total = call(
        gather_kernel,
        tile_list,
        [SMEM] + [VMEM] * 3,
        (send_tiles, own, from_second, from_first),
    )
    smooth, second, first = call(
        complete_kernel,
        (narrow_list, four, four),
        [VMEM] * 4,
        (send_tiles, total, payload, arrived),
        [pltpu.VMEM((tiles,) + tile_shape, F32), links, sem],
    )
    from_second = swap(second, 2)
    from_first = swap(first, 0)
    partial = call(
        own_forward_kernel, shape((rows, wide), F32), [VMEM] * 2, (smooth, own_blocks)
    )
    return call(
        forward_kernel,
        shape(fields.shape, F32),
        [VMEM] * 7,
        (partial, second, first, from_second, from_first, received_blocks, interp),
        [pltpu.VMEM((rows, wide), BF16), pltpu.VMEM((rows, wide), BF16)],
    )


def solution(mesh):
    in_specs = (
        P(None, "lev", "patch"),
        P("patch", None, None),
        P("patch", None, None, None),
        P(),
        P("patch", None, None),
        P("patch", None),
    )
    out_specs = P(None, "lev", "patch")
    return jax.shard_map(shards, mesh=mesh, in_specs=in_specs, out_specs=out_specs, check_vma=False)
```
